32 devices in a mesh: stream: 2 (over y), pairs: 16 (over z, x, core).
Axes of the slice: x: 2, y: 2, z: 4, core: 2. Of those that a mesh axis runs over, the one named last changes fastest.
Arguments:
- tokens: bfloat16 [2, 2, 8192, 768], P('stream', None, 'pairs'), may hold values from -6 to 6
- segments: int32 [2, 2, 16, 512], P('stream', None, 'pairs'), may hold values from 0 to 3, never falling along the last dimension, each value on 1 to 384 neighbouring positions
- counts: int32 [2, 16], replicated, may hold values from 2 to 4
- cotangent: bfloat16 [2, 2, 8192, 768], P('stream', None, 'pairs'), may hold values from -6 to 6
- w_query: bfloat16 [768, 768], replicated, may hold values from -0.21875 to 0.21875
- b_query: bfloat16 [768], replicated, may hold values from -3 to 3
- w_key: bfloat16 [768, 768], replicated, may hold values from -0.21875 to 0.21875
- w_value: bfloat16 [768, 768], replicated, may hold values from -0.21875 to 0.21875
- b_value: bfloat16 [768], replicated, may hold values from -3 to 3
- w_out: bfloat16 [768, 768], replicated, may hold values from -0.875 to 0.875
- b_out: bfloat16 [768], replicated, may hold values from -2 to 2
- gain_attn: bfloat16 [768], replicated, may hold values from 0.5 to 1.5
- bias_attn: bfloat16 [768], replicated, may hold values from -1.5 to 1.5
- w_inner: bfloat16 [768, 3072], replicated, may hold values from -0.21875 to 0.21875
- b_inner: bfloat16 [3072], replicated, may hold values from -3 to 3
- w_outer: bfloat16 [3072, 768], replicated, may hold values from -0.109375 to 0.109375
- b_outer: bfloat16 [768], replicated, may hold values from -2 to 2
- gain_ffn: bfloat16 [768], replicated, may hold values from 0.5 to 1.5
- bias_ffn: bfloat16 [768], replicated, may hold values from -0.796875 to 0.796875
Outputs:
- loss_rows: float32 [2, 2, 64], P('stream', None, 'pairs')
- embeddings: float32 [2, 2, 64, 768], P('stream', None, 'pairs')
- embedding_grads: float32 [2, 2, 64, 768], P('stream', None, 'pairs')
- hidden_states: bfloat16 [2, 2, 8192, 768], P('stream', None, 'pairs')
- token_grads: bfloat16 [2, 2, 8192, 768], P('stream', None, 'pairs')
- grad_w_query: float32 [768, 768], replicated
- grad_b_query: float32 [768], replicated
- grad_w_key: float32 [768, 768], replicated
- grad_w_value: float32 [768, 768], replicated
- grad_b_value: float32 [768], replicated
- grad_w_out: float32 [768, 768], replicated
- grad_b_out: float32 [768], replicated
- grad_gain_attn: float32 [768], replicated
- grad_bias_attn: float32 [768], replicated
- grad_w_inner: float32 [768, 3072], replicated
- grad_b_inner: float32 [3072], replicated
- grad_w_outer: float32 [3072, 768], replicated
- grad_b_outer: float32 [768], replicated
- grad_gain_ffn: float32 [768], replicated
- grad_bias_ffn: float32 [768], replicated
The draws below stay inside these ranges and needn't reach their ends.
All inputs are finite; a program needn't handle non-finite values.
Results may differ from the reference program's by a relative error of at most 0.014.
Values sent between devices are 32-bit elements; how exact they have to be, the bound alone decides.
No kernel may reach another device: no remote copies, remote signals or barrier semaphores. Data moves between devices by JAX's collectives and lax.ppermute only.
A program may use at most 256 MiB of HBM per device.

```python
import math
import jax
import jax.numpy as jnp
import numpy as np
from jax import lax

D = 768
HEADS = 12
HEAD_DIM = 64
FF = 3072
P_SIZE = 512
SLOTS = 4
MB = 2
MOST = 384
TOKENS = 8192
N_ALL = 64
N_PAIRS = 16


def plant(drawn, rng, smallest, largest):
    index_at = [jax.random.randint(jax.random.fold_in(rng, axis), (), 0, length) for axis, length in enumerate(drawn.shape)]
    main_axis = drawn.shape.index(max(drawn.shape))
    beside = index_at[:main_axis] + [(index_at[main_axis] + 1) % drawn.shape[main_axis]] + index_at[main_axis + 1:]
    return drawn.at[tuple(index_at)].set(smallest).at[tuple(beside)].set(largest)


def levels(rng, dims, pieces, smallest, top_value):
    def one(dim, blocks):
        heights = jax.random.uniform(jax.random.fold_in(jax.random.fold_in(rng, 6), dim), (blocks,), jnp.float32, smallest / len(pieces), top_value / len(pieces))
        return jnp.repeat(jnp.exp(heights), dims[dim] // blocks).reshape((-1,) + (1,) * (len(dims) - dim - 1))

    factor_of = one(*pieces[0])
    for cut in pieces[1:]:
        factor_of = factor_of * one(*cut)
    return factor_of


def split_up(number_of, total, most, slope):
    portions = [(1 << 20) // math.isqrt(standing ** slope) + 1 for standing in range(2, number_of + 1)]
    spare, given = total - most - (number_of - 1), [1] * (number_of - 1)
    while spare > 0:
        free = [i for i in range(number_of - 1) if given[i] < most]
        whole, left = sum([portions[i] for i in free]), spare
        for i in free:
            extra = min(most - given[i], max(1, left * portions[i] // whole), spare)
            given[i] = given[i] + extra
            spare = spare - extra
    return np.array([most] + given)


def uneven(rng, count, total, bound, skew):
    if count == 2:
        one = jax.random.randint(rng, (), max(1, total - bound), min(bound, total - 1) + 1)
        return jnp.stack([one, total - one])
    sizes = jnp.asarray(split_up(count, total, bound, skew), jnp.int32)
    twos = (count - 1) // 2
    donor, receiver = sizes[1:1 + 2 * twos:2], sizes[2:2 + 2 * twos:2]
    slack = jnp.minimum(donor - 1, bound - receiver)
    shifted = jax.random.randint(jax.random.fold_in(rng, 1), (twos,), 0, 1 << 20) % (slack + 1)
    sizes = sizes.at[1:1 + 2 * twos:2].set(donor - shifted).at[2:2 + 2 * twos:2].set(receiver + shifted)
    return sizes[jax.random.permutation(jax.random.fold_in(rng, 2), count)]


def bell_draw(own_key, shape, width, reach, pieces=(), held_as=jnp.bfloat16):
    entries = jax.random.normal(own_key, shape, jnp.float32) * width
    if len(pieces) > 0:
        entries = levels(own_key, shape, pieces, -0.22, 0.18) * entries
    return jnp.clip(entries, min=-reach, max=reach).astype(held_as)


def setup_inputs(seed: int = 0) -> dict:
    seeds = jax.random.split(jax.random.key(seed), 20)
    tokens = bell_draw(seeds[0], (2, MB, TOKENS, D), 1.0, 6.0, ((0, 2), (2, 16)))
    segments = jax.vmap(lambda own: jnp.searchsorted(jnp.cumsum(uneven(own, SLOTS, P_SIZE, MOST, 1)), jnp.arange(P_SIZE), side="right"))(jax.random.split(seeds[1], 2 * MB * N_PAIRS)).reshape((2, MB, N_PAIRS, P_SIZE)).astype(jnp.int32)
    counts = plant(jax.random.randint(seeds[2], (MB, N_PAIRS), 2, SLOTS + 1), jax.random.fold_in(seeds[2], 1), 2, SLOTS).astype(jnp.int32)
    cotangent = bell_draw(seeds[3], (2, MB, TOKENS, D), 1.0, 6.0, ((0, 2), (2, 16)))
    w_query = bell_draw(seeds[4], (D, D), D ** -0.5, 0.21875)
    b_query = bell_draw(seeds[5], (D,), 0.5, 3.0)
    w_key = bell_draw(seeds[6], (D, D), D ** -0.5, 0.21875)
    w_value = bell_draw(seeds[7], (D, D), D ** -0.5, 0.21875)
    b_value = bell_draw(seeds[8], (D,), 0.5, 3.0)
    w_out = bell_draw(seeds[9], (D, D), (D // 16) ** -0.5, 0.875)
    b_out = bell_draw(seeds[10], (D,), 0.3, 2.0)
    gain_attn = jnp.clip(1.0 + 0.1 * jax.random.normal(seeds[11], (D,), jnp.float32), 0.5, 1.5).astype(jnp.bfloat16)
    bias_attn = bell_draw(seeds[12], (D,), 0.2, 1.5)
    w_inner = bell_draw(seeds[13], (D, FF), D ** -0.5, 0.21875)
    b_inner = bell_draw(seeds[14], (FF,), 0.5, 3.0)
    w_outer = bell_draw(seeds[15], (FF, D), FF ** -0.5, 0.109375)
    b_outer = bell_draw(seeds[16], (D,), 0.3, 2.0)
    gain_ffn = jnp.clip(1.0 + 0.1 * jax.random.normal(seeds[17], (D,), jnp.float32), 0.5, 1.5).astype(jnp.bfloat16)
    bias_ffn = bell_draw(seeds[18], (D,), 0.1, 0.796875)
    return dict(tokens=tokens, segments=segments, counts=counts, cotangent=cotangent, w_query=w_query, b_query=b_query, w_key=w_key, w_value=w_value, b_value=b_value, w_out=w_out, b_out=b_out, gain_attn=gain_attn, bias_attn=bias_attn, w_inner=w_inner, b_inner=b_inner, w_outer=w_outer, b_outer=b_outer, gain_ffn=gain_ffn, bias_ffn=bias_ffn)


HIGHEST = lax.Precision.HIGHEST
LOGIT_DIVISOR = 0.01
NORM_EPS = 1e-12
UNIT_EPS = 1e-06

@jax.custom_vjp
def low(v):
    return lax.optimization_barrier(v.astype(jnp.bfloat16)).astype(jnp.float32)

@jax.custom_vjp
def low_back(v):
    return v

def low_keep(v):
    return (low(v), None)

def low_pass(kept, grad):
    return (grad,)

def back_keep(v):
    return (v, None)

def back_low(kept, grad):
    return (low(grad),)
low.defvjp(low_keep, low_pass)
low_back.defvjp(back_keep, back_low)

def dense_multiply(left, right):
    return jnp.dot(left, right, precision=HIGHEST, preferred_element_type=jnp.float32)

def layer_norm(total, norm_gain, layer_offset):
    centered = total - lax.optimization_barrier(jnp.mean(total, axis=-1, keepdims=True))
    variance = lax.optimization_barrier(jnp.mean(centered * centered, axis=-1, keepdims=True))
    return centered * lax.rsqrt(variance + NORM_EPS) * norm_gain + layer_offset

def unit_scale(pooled):
    return pooled * lax.rsqrt(lax.optimization_barrier(jnp.mean(pooled * pooled, axis=-1, keepdims=True)) + UNIT_EPS) * D ** (-0.5)

def pack_layer(inputs, segment, params):
    w_query, b_query, w_key, w_value, b_value, w_out, b_out, gain_attn, bias_attn, w_inner, b_inner, w_outer, b_outer, gain_ffn, bias_ffn = params
    length = inputs.shape[0]
    queries = low(low_back(dense_multiply(inputs, w_query)) + b_query).reshape(length, HEADS, HEAD_DIM)
    keys = low(low_back(dense_multiply(inputs, w_key))).reshape(length, HEADS, HEAD_DIM)
    values = low(low_back(dense_multiply(inputs, w_value)) + b_value).reshape(length, HEADS, HEAD_DIM)
    raw_scores = jnp.einsum('qhd,khd->hqk', queries, keys, precision=HIGHEST) * HEAD_DIM ** (-0.5)
    same_segment = segment[:, None] == segment[None, :]
    scores = jnp.where(same_segment[None], low_back(raw_scores), -1000000000.0)
    probs = low(jax.nn.softmax(scores, axis=-1))
    mixed = low(low_back(jnp.einsum('hqk,khd->qhd', probs, values, precision=HIGHEST))).reshape(length, D)
    attended = low_back(dense_multiply(mixed, w_out)) + b_out
    first = layer_norm(inputs + attended, gain_attn, bias_attn)
    inner = low_back(dense_multiply(low(first), w_inner)) + b_inner
    activated = low(jax.nn.gelu(inner, approximate=False))
    outer = low_back(dense_multiply(activated, w_outer)) + b_outer
    hidden = layer_norm(first + outer, gain_ffn, bias_ffn)
    one_hot = (segment[None, :] == jnp.arange(SLOTS, dtype=jnp.int32)[:, None]).astype(jnp.float32)
    counted = lax.optimization_barrier(jnp.sum(one_hot, axis=1, keepdims=True))
    pooled = dense_multiply(one_hot, hidden) / counted
    return (hidden, unit_scale(pooled))

def contrast_objective(units, counts):
    column_ids = jnp.arange(N_ALL, dtype=jnp.int32)

    def batch_loss(query_vectors, passage_vectors, count_row):
        column_valid = column_ids % SLOTS < jnp.repeat(count_row, SLOTS)
        cosine_scores = dense_multiply(query_vectors, passage_vectors.T) / LOGIT_DIVISOR
        masked = jnp.where(column_valid[None, :], cosine_scores, -1000000000.0)
        totals = jax.nn.logsumexp(masked, axis=-1)
        return (totals - jnp.diagonal(cosine_scores)) * column_valid.astype(jnp.float32)
    stream_rows = []
    for stream_number in range(2):
        batch_rows = []
        for batch_number in range(MB):
            batch_rows.append(batch_loss(units[stream_number, batch_number], units[1 - stream_number, batch_number], counts[batch_number]))
        stream_rows.append(jnp.stack(batch_rows))
    return jnp.stack(stream_rows)

def reference(tokens, segments, counts, cotangent, w_query, b_query, w_key, w_value, b_value, w_out, b_out, gain_attn, bias_attn, w_inner, b_inner, w_outer, b_outer, gain_ffn, bias_ffn):
    params = tuple((weight.astype(jnp.float32) for weight in (w_query, b_query, w_key, w_value, b_value, w_out, b_out, gain_attn, bias_attn, w_inner, b_inner, w_outer, b_outer, gain_ffn, bias_ffn)))
    packs = 2 * MB * N_PAIRS
    inputs = tokens.astype(jnp.float32).reshape(packs, P_SIZE, D)
    pack_segments = segments.reshape(packs, P_SIZE)

    def forward(inputs_all, params_all):

        def one_pack(carried):
            return pack_layer(carried[0], carried[1], params_all)
        return lax.map(jax.checkpoint(one_pack), (inputs_all, pack_segments))
    (hidden, units), layer_back = jax.vjp(forward, inputs, params)
    units_all = units.reshape(2, MB, N_ALL, D)
    losses, loss_back = jax.vjp(lambda held: contrast_objective(held, counts), units_all)
    unit_grads, = loss_back(jnp.ones_like(losses))
    grad_inputs, grad_params = layer_back((cotangent.astype(jnp.float32).reshape(packs, P_SIZE, D), unit_grads.reshape(packs, SLOTS, D)))
    return (losses, units_all, unit_grads, hidden.reshape(2, MB, TOKENS, D).astype(jnp.bfloat16), grad_inputs.reshape(2, MB, TOKENS, D).astype(jnp.bfloat16), grad_params[0], grad_params[1], grad_params[2], grad_params[3], grad_params[4], grad_params[5], grad_params[6], grad_params[7], grad_params[8], grad_params[9], grad_params[10], grad_params[11], grad_params[12], grad_params[13], grad_params[14])
```

```python
import functools
import jax
import jax.numpy as jnp
import numpy as np
from jax import lax
from jax.experimental import pallas as pl
from jax.experimental.pallas import tpu as pltpu
from jax.sharding import PartitionSpec as P

D = 768
HEADS = 12
HEAD_DIM = 64
SLOTS = 4
AXES = ("stream", "pairs")
F32 = jnp.float32
BF16 = jnp.bfloat16
HIGHEST = lax.Precision.HIGHEST
LOGIT_DIVISOR = 0.01
NORM_EPS = 1e-12
UNIT_EPS = 1e-06
NEG = -1000000000.0
SCALE = HEAD_DIM**-0.5
FF_CHUNK = 512
MIB = 1 << 20

TAIL_P = 0.305
TAIL = (
    0.12163973223592059,
    0.12246682364852957,
    0.10342082369335875,
    0.12102182071723708,
    -0.03797709812500149,
    0.18571719569775694,
    -0.15298848174013205,
    0.0366992308655468,
)


def dims(lhs, rhs, contract, **kw):
    return lax.dot_general(lhs, rhs, (contract, ((), ())), preferred_element_type=F32, **kw)


def matmul(lhs, rhs):
    return dims(lhs, rhs, ((1,), (0,)))


def matmul_nt(lhs, rhs):
    return dims(lhs, rhs, ((1,), (1,)))


def matmul_tn(lhs, rhs):
    return dims(lhs, rhs, ((0,), (0,)))


def norm_forward(total):
    centered = total - jnp.mean(total, axis=-1, keepdims=True)
    inv_std = lax.rsqrt(jnp.mean(centered * centered, axis=-1, keepdims=True) + NORM_EPS)
    return centered * inv_std, inv_std


def gelu_both(x):
    tail = 1.0 / (1.0 + TAIL_P * jnp.abs(x))
    poly = jnp.full_like(x, TAIL[-1])
    for coefficient in TAIL[-2::-1]:
        poly = poly * tail + coefficient
    bell = jnp.exp(-0.5 * (x * x))
    lower = poly * tail * bell
    phi = jnp.where(x >= 0, 1.0 - lower, lower)
    return x * phi, phi + x * bell * 0.3989422804014327


def segment_mask(seg_row):
    length = seg_row.shape[1]
    rows = jnp.broadcast_to(seg_row.astype(F32), (128, length))
    columns = rows.T
    wide = jnp.concatenate([columns] * (length // 128), axis=1)
    return jnp.where(wide == jnp.broadcast_to(seg_row.astype(F32), (length, length)), 0.0, NEG)


def forward_kernel(
    tokens, seg, wq, bq, wk, wv, bv, wo, bo, g1, c1, bi, bo2, g2, c2, wi_hbm, wo2_hbm,
    q_out, k_out, v_out, mixed_out, stat_out, first_out, normed1_out, act_out, slope_out,
    normed2_out, hidden_out, pooled_out, unit_out,
    wi, wo2, mask, first_f32, acc, sem,
):
    copy_in = pltpu.make_async_copy(wi_hbm, wi, sem.at[0])
    copy_out = pltpu.make_async_copy(wo2_hbm, wo2, sem.at[1])

    @pl.when(pl.program_id(0) == 0)
    def _():
        copy_in.start()
        copy_out.start()

    x = tokens[...]
    length = x.shape[0]
    q_out[...] = (matmul(x, wq[...]) + bq[...].astype(F32)).astype(BF16)
    k_out[...] = matmul(x, wk[...]).astype(BF16)
    v_out[...] = (matmul(x, wv[...]) + bv[...].astype(F32)).astype(BF16)
    mask[...] = segment_mask(seg[...])
    low_half = lax.broadcasted_iota(jnp.int32, (length, 128), 1) < HEAD_DIM

    def head_pair(pair, carry):
        lanes = pl.ds(pl.multiple_of(pair * 128, 128), 128)
        q2 = q_out[:, lanes] * BF16(SCALE)
        k2 = k_out[:, lanes]
        v2 = v_out[:, lanes].astype(F32).T.astype(BF16)
        outs = []
        for h in range(2):
            kh = jnp.where(low_half if h == 0 else ~low_half, k2, BF16(0))
            s = matmul_nt(kh, q2) + mask[...]
            top = jnp.max(s, axis=0, keepdims=True)
            e = jnp.exp(s - top)
            total = jnp.sum(e, axis=0, keepdims=True)
            o = matmul(v2[h * HEAD_DIM : (h + 1) * HEAD_DIM], e.astype(BF16)) * (1.0 / total)
            outs.append(o)
            stat_out[pl.ds(pair * 2 + h, 1), :] = top + jnp.log(total)
        mixed_out[:, lanes] = jnp.concatenate(outs, axis=0).T.astype(BF16)
        return carry

    lax.fori_loop(0, HEADS // 2, head_pair, 0)
    total = x.astype(F32) + (matmul(mixed_out[...], wo[...]) + bo[...].astype(F32))
    normed1, inv1 = norm_forward(total)
    normed1_out[...] = normed1.astype(normed1_out.dtype)
    first = normed1 * g1[...].astype(F32) + c1[...].astype(F32)
    first_f32[...] = first
    first_out[...] = first.astype(BF16)

    @pl.when(pl.program_id(0) == 0)
    def _():
        copy_in.wait()
        copy_out.wait()

    acc[...] = jnp.zeros_like(acc)

    def ff_chunk(c, carry):
        lanes = pl.ds(pl.multiple_of(c * FF_CHUNK, FF_CHUNK), FF_CHUNK)
        inner = matmul(first_out[...], wi[:, lanes]) + bi[:, lanes].astype(F32)
        act, slope = gelu_both(inner)
        act = act.astype(BF16)
        act_out[:, lanes] = act
        slope_out[:, lanes] = slope.astype(slope_out.dtype)
        acc[...] += matmul(act, wo2[lanes, :])
        return carry

    lax.fori_loop(0, wi.shape[1] // FF_CHUNK, ff_chunk, 0)
    normed2, inv2 = norm_forward(first_f32[...] + (acc[...] + bo2[...].astype(F32)))
    normed2_out[...] = normed2.astype(normed2_out.dtype)
    hidden = normed2 * g2[...].astype(F32) + c2[...].astype(F32)
    hidden_out[...] = hidden.astype(BF16)
    slots = lax.broadcasted_iota(jnp.int32, (8, length), 0)
    one_hot = jnp.where(jnp.broadcast_to(seg[...], (8, length)) == slots, 1.0, 0.0)
    counted = jnp.maximum(jnp.sum(one_hot, axis=1, keepdims=True), 1.0)
    pooled = dims(one_hot, hidden, ((1,), (0,)), precision=HIGHEST) / counted
    pooled = pooled[:SLOTS]
    pooled_out[...] = pooled
    unit_out[...] = (
        pooled * lax.rsqrt(jnp.mean(pooled * pooled, axis=-1, keepdims=True) + UNIT_EPS) * D**-0.5
    )
    stat_out[pl.ds(HEADS, 1), :] = jnp.broadcast_to(inv1, (length, 128)).T[:1]
    stat_out[pl.ds(HEADS + 1, 1), :] = jnp.broadcast_to(inv2, (length, 128)).T[:1]


def forward(tokens, segments, w):
    batches, length, _ = tokens.shape
    ff = w["inner"].shape[1]

    def per_batch(rows, cols):
        return pl.BlockSpec((None, rows, cols), lambda b: (b, 0, 0))

    def whole(a):
        return pl.BlockSpec(a.shape, lambda b: (0,) * a.ndim, pipeline_mode=pl.Buffered(1))

    hbm = pl.BlockSpec(memory_space=pl.ANY)
    vec = lambda a: a.reshape(1, -1)
    small = [
        w["query"], vec(w["b_query"]), w["key"], w["value"], vec(w["b_value"]), w["out"],
        vec(w["b_out"]), vec(w["gain1"]), vec(w["shift1"]), vec(w["b_inner"]), vec(w["b_outer"]),
        vec(w["gain2"]), vec(w["shift2"]),
    ]
    outs = [
        (length, D, BF16), (length, D, BF16), (length, D, BF16), (length, D, BF16),
        (16, length, F32), (length, D, BF16), (length, D, BF16), (length, ff, BF16),
        (length, ff, BF16), (length, D, BF16), (length, D, BF16), (SLOTS, D, F32), (SLOTS, D, F32),
    ]
    return pl.pallas_call(
        forward_kernel,
        grid=(batches,),
        in_specs=[per_batch(length, D), per_batch(1, length)] + [whole(a) for a in small] + [hbm, hbm],
        out_specs=[per_batch(r, c) for r, c, _ in outs],
        out_shape=[jax.ShapeDtypeStruct((batches, r, c), t) for r, c, t in outs],
        scratch_shapes=[
            pltpu.VMEM((D, ff), BF16),
            pltpu.VMEM((ff, D), BF16),
            pltpu.VMEM((length, length), F32),
            pltpu.VMEM((length, D), F32),
            pltpu.VMEM((length, D), F32),
            pltpu.SemaphoreType.DMA((2,)),
        ],
        compiler_params=pltpu.CompilerParams(vmem_limit_bytes=60 * MIB),
        name="forward_layer",
    )(tokens, segments, *small, w["inner"], w["outer"])


def attention_backward_kernel(q, k, v, do, stat, seg, dq_out, dk_out, dv_out, sums_out, mask):
    length = q.shape[0]
    mask[...] = segment_mask(seg[...])
    low_half = lax.broadcasted_iota(jnp.int32, (length, 128), 1) < HEAD_DIM

    def head_pair(pair, carry):
        lanes = pl.ds(pl.multiple_of(pair * 128, 128), 128)
        q2 = q[:, lanes] * BF16(SCALE)
        k2 = k[:, lanes]
        v2 = v[:, lanes]
        do2 = do[:, lanes]
        k2t = (k2.astype(F32) * SCALE).T.astype(BF16)
        dqs, dks, dvs = [], [], []
        for h in range(2):
            half = low_half if h == 0 else ~low_half
            s = matmul_nt(jnp.where(half, k2, BF16(0)), q2) + mask[...]
            p = jnp.exp(s - stat[pl.ds(pair * 2 + h, 1), :])
            dp = matmul_nt(jnp.where(half, v2, BF16(0)), do2)
            pdp = p * dp
            delta = jnp.sum(pdp, axis=0, keepdims=True)
            ds = (pdp - p * delta).astype(BF16)
            dvs.append(matmul(p.astype(BF16), do2))
            dks.append(matmul(ds, q2))
            dqs.append(matmul(k2t[h * HEAD_DIM : (h + 1) * HEAD_DIM], ds))
        dq = jnp.concatenate(dqs, axis=0).T
        dk = jnp.where(low_half, dks[0], dks[1])
        dv = jnp.where(low_half, dvs[0], dvs[1])
        dq_out[:, lanes] = dq.astype(BF16)
        dk_out[:, lanes] = dk.astype(BF16)
        dv_out[:, lanes] = dv.astype(BF16)
        sums_out[0:1, lanes] = jnp.sum(dq, axis=0, keepdims=True)
        sums_out[1:2, lanes] = jnp.sum(dv, axis=0, keepdims=True)
        return carry

    lax.fori_loop(0, HEADS // 2, head_pair, 0)


def attention_backward(q, k, v, do, stat, segments):
    batches, length, _ = q.shape

    def per_batch(rows, cols):
        return pl.BlockSpec((None, rows, cols), lambda b: (b, 0, 0))

    wide = per_batch(length, D)
    shape = jax.ShapeDtypeStruct(q.shape, BF16)
    return pl.pallas_call(
        attention_backward_kernel,
        grid=(batches,),
        in_specs=[wide, wide, wide, wide, per_batch(16, length), per_batch(1, length)],
        out_specs=[wide, wide, wide, per_batch(8, D)],
        out_shape=[shape, shape, shape, jax.ShapeDtypeStruct((batches, 8, D), F32)],
        scratch_shapes=[pltpu.VMEM((length, length), F32)],
        compiler_params=pltpu.CompilerParams(vmem_limit_bytes=48 * MIB),
        name="attention_backward",
    )(q, k, v, do, stat, segments)


def contrast_kernel(
    place, every, own, pooled, counted, valid_row, valid_col, loss_out, grad_out, pooled_grad_out
):
    rows = every.shape[0]
    everything = every[...]
    mine = own[...]

    def batch_of(r):
        return (r >> 2) & 1

    streams_col, streams_row = valid_col[1], valid_row[1:2, :]
    ok_col, ok_row = valid_col[0], valid_row[0:1, :]
    r_col = lax.broadcasted_iota(jnp.int32, (rows, 1), 0)
    r_row = lax.broadcasted_iota(jnp.int32, (1, rows), 1)
    logits = dims(everything, everything, ((1,), (1,)), precision=HIGHEST) / LOGIT_DIVISOR
    related = (batch_of(r_col) == batch_of(r_row)) & (streams_col != streams_row) & (ok_col > 0)
    masked = jnp.where(related, logits, NEG)
    top = jnp.max(masked, axis=0, keepdims=True)
    lse_row = top + jnp.log(jnp.sum(jnp.exp(masked - top), axis=0, keepdims=True))

    o_col = lax.broadcasted_iota(jnp.int32, (8, 1), 0)
    my_stream = place[1].astype(F32)
    my_partner = place[2] * 8 + o_col
    mine_at = place[0] * 8 + o_col
    my_valid = jnp.sum(jnp.where(r_row == mine_at, ok_row, 0.0), axis=1, keepdims=True)
    own_logits = dims(mine, everything, ((1,), (1,)), precision=HIGHEST) / LOGIT_DIVISOR
    other = (batch_of(o_col) == batch_of(r_row)) & (streams_row != my_stream)
    target = jnp.where(r_row == my_partner, 1.0, 0.0)
    forward_logits = jnp.where(other & (ok_row > 0), own_logits, NEG)
    own_top = jnp.max(forward_logits, axis=1, keepdims=True)
    own_lse = own_top + jnp.log(
        jnp.sum(jnp.exp(forward_logits - own_top), axis=1, keepdims=True)
    )
    loss = (own_lse - jnp.sum(target * own_logits, axis=1, keepdims=True)) * my_valid
    loss_out[...] = jnp.broadcast_to(loss, loss_out.shape)
    forward_grad = (jnp.exp(forward_logits - own_lse) - target) * my_valid
    back_logits = jnp.where(other & (my_valid > 0), own_logits, NEG)
    back_grad = jnp.where(other, (jnp.exp(back_logits - lse_row) - target) * ok_row, 0.0)
    both = (forward_grad + back_grad) / LOGIT_DIVISOR
    grad = dims(both, everything, ((1,), (0,)), precision=HIGHEST)
    grad_out[...] = grad
    pool = pooled[...]
    inv = lax.rsqrt(jnp.mean(pool * pool, axis=-1, keepdims=True) + UNIT_EPS)
    through = grad * D**-0.5
    inner = jnp.mean(pool * through, axis=-1, keepdims=True)
    pooled_grad_out[...] = (through * inv - pool * (inner * inv * inv * inv)) / counted[...]


def contrast(place, every, own, pooled, counted, valid_row, valid_col):
    rows = every.shape[0]
    smem = pl.BlockSpec(memory_space=pltpu.SMEM)
    vmem = pl.BlockSpec(memory_space=pltpu.VMEM)
    return pl.pallas_call(
        contrast_kernel,
        in_specs=[smem] + [vmem] * 6,
        out_specs=[vmem] * 3,
        out_shape=[
            jax.ShapeDtypeStruct((8, 128), F32),
            jax.ShapeDtypeStruct((8, D), F32),
            jax.ShapeDtypeStruct((8, D), F32),
        ],
        compiler_params=pltpu.CompilerParams(vmem_limit_bytes=40 * MIB),
        name="contrast",
    )(place, every, own, pooled, counted, valid_row, valid_col)


def stages(pairs):
    bits = pairs.bit_length() - 1
    p = lax.axis_index("pairs")
    s = lax.axis_index("stream")
    core = p & 1

    def table(move):
        return [
            (a * pairs + b, move(a, b)[0] * pairs + move(a, b)[1])
            for a in range(2)
            for b in range(pairs)
        ]

    made = {
        "core": (core, table(lambda a, b: (a, b ^ 1))),
        "xy": (
            jnp.where(core == 0, (p >> 1) & 1, s),
            table(lambda a, b: (a, b ^ 2) if b % 2 == 0 else (a ^ 1, b)),
        ),
        "yx": (
            jnp.where(core == 0, s, (p >> 1) & 1),
            table(lambda a, b: (a ^ 1, b) if b % 2 == 0 else (a, b ^ 2)),
        ),
    }
    for n in range(2, bits):
        made[n] = ((p >> n) & 1, table(lambda a, b, n=n: (a, b ^ (1 << n))))
    return made


def send(value, permutation):
    return lax.ppermute(value, AXES, permutation)


def gather_all(value, steps, order):
    for name in order:
        bit, permutation = steps[name]
        got = send(value, permutation)
        value = jnp.concatenate(
            [jnp.where(bit == 0, value, got), jnp.where(bit == 0, got, value)], axis=0
        )
    return value


def gather_layout(pairs, order):
    blocks = []
    for block in range(2 * pairs):
        bit = {name: (block >> at) & 1 for at, name in enumerate(order)}
        core = bit["core"]
        x, s = (bit["xy"], bit["yx"]) if core == 0 else (bit["yx"], bit["xy"])
        pair = core + 2 * x
        for name in order:
            if isinstance(name, int):
                pair += bit[name] << name
        blocks.append((s, pair))
    return np.array(blocks)


def sum_of(terms):
    total = terms[0]
    for term in terms[1:]:
        total = total + term
    return total


def half_of(terms, which):
    rows = terms[0].shape[0] // 2
    return [lax.dynamic_slice_in_dim(term, which * rows, rows, 0) for term in terms]


def grouped(jobs):
    groups = {}
    for at, (_, name) in enumerate(jobs):
        groups.setdefault(name, []).append(at)
    return groups.items()


def transfer(buffers, permutation):
    if len(buffers) == 1:
        return [send(buffers[0], permutation)]
    got = send(jnp.concatenate(buffers, axis=0), permutation)
    parts, start = [], 0
    for buffer in buffers:
        parts.append(got[start : start + buffer.shape[0]])
        start += buffer.shape[0]
    return parts


def scatter_step(steps, jobs, extra=None):
    done = [None] * len(jobs)
    for name, members in grouped(jobs):
        bit, permutation = steps[name]
        buffers = [sum_of(half_of(jobs[at][0], 1 - bit)) for at in members]
        riding = extra is not None and 0 in members
        got = transfer(buffers + ([extra] if riding else []), permutation)
        for at, part in zip(members, got):
            done[at] = [sum_of(half_of(jobs[at][0], bit)), part]
        if riding:
            summed = extra + got[-1]
    return (done, summed) if extra is not None else done


def swap_step(steps, values, name):
    got = transfer(values, steps[name][1])
    return [value + part for value, part in zip(values, got)]


def collect_step(steps, jobs):
    done = [None] * len(jobs)
    for name, members in grouped(jobs):
        bit, permutation = steps[name]
        buffers = [jobs[at][0] for at in members]
        for at, buffer, part in zip(members, buffers, transfer(buffers, permutation)):
            done[at] = jnp.concatenate(
                [jnp.where(bit == 0, buffer, part), jnp.where(bit == 0, part, buffer)], axis=0
            )
    return done


def sum_over_devices(grad, pairs, steps, extra=None):
    bits = pairs.bit_length() - 1
    tail = list(range(3, bits - 1))
    last = bits - 1
    wide_order = ["core", "xy", "yx", 2] + tail
    deep_order = ["core", 2, "yx", "xy"] + tail
    cut = grad.shape[0] * 2 // 3
    wide, deep = [grad[:cut]], [grad[cut:]]
    for a, b in zip(wide_order, deep_order):
        jobs = [(wide, a), (deep, b)]
        if extra is None:
            wide, deep = scatter_step(steps, jobs)
        else:
            (wide, deep), extra = scatter_step(steps, jobs, extra)
    values = [sum_of(wide), sum_of(deep)] + ([] if extra is None else [extra])
    values = swap_step(steps, values, last)
    wide, deep = values[:2]
    for a, b in zip(wide_order[::-1], deep_order[::-1]):
        wide, deep = collect_step(steps, [(wide, a), (deep, b)])
    total = jnp.concatenate([wide, deep], axis=0)
    return total if extra is None else (total, values[2])


def on_device(
    tokens, segments, counts, cotangent, w_query, b_query, w_key, w_value, b_value, w_out, b_out,
    gain_attn, bias_attn, w_inner, b_inner, w_outer, b_outer, gain_ffn, bias_ffn,
):
    pairs = lax.axis_size("pairs")
    bits = pairs.bit_length() - 1
    batches, length = tokens.shape[1], tokens.shape[2]
    ff = w_inner.shape[1]
    stream = lax.axis_index("stream")
    pair = lax.axis_index("pairs")
    steps = stages(pairs)
    w = dict(
        query=w_query, b_query=b_query, key=w_key, value=w_value, b_value=b_value, out=w_out,
        b_out=b_out, gain1=gain_attn, shift1=bias_attn, inner=w_inner, b_inner=b_inner,
        outer=w_outer, b_outer=b_outer, gain2=gain_ffn, shift2=bias_ffn,
    )
    x = tokens[0]
    seg = segments[0]
    order = list(range(bits - 1, 1, -1)) + ["xy", "yx", "core"]
    layout = gather_layout(pairs, order)
    slot = jnp.arange(SLOTS, dtype=jnp.int32)
    block_counts = counts[:, layout[:, 1]].T
    valid = (slot[None, None, :] < block_counts[:, :, None]).astype(F32).reshape(-1)
    streams = jnp.asarray(np.repeat(layout[:, 0], batches * SLOTS), F32)
    valid_row = jnp.stack([valid, streams])
    valid_col = valid_row[:, :, None]
    block_of = np.zeros((2, pairs), np.int32)
    for block, (s, p) in enumerate(layout):
        block_of[s, p] = block
    own_block = jnp.asarray(block_of)[stream, pair]
    partner_block = jnp.asarray(block_of)[1 - stream, pair]
    place = jnp.stack([own_block, stream, partner_block]).astype(jnp.int32)
    one_hot = (seg[:, 0, None, :] == slot[None, :, None]).astype(F32)
    counted = jnp.sum(one_hot, axis=2).reshape(batches * SLOTS, 1)

    (q, k, v, mixed, stat, first_low, normed1, act, slope, normed2, hidden, pooled, unit) = forward(
        x, seg, w
    )
    unit = unit.reshape(batches * SLOTS, D)
    every = gather_all(unit, steps, order)
    loss, unit_grad, pooled_grad = contrast(
        place, every, unit, pooled.reshape(batches * SLOTS, D), counted, valid_row, valid_col
    )
    loss = loss[:, 0].reshape(1, batches, SLOTS)

    tokens_all = batches * length
    flat = lambda a: a.reshape(tokens_all, a.shape[-1])
    inv1 = stat[:, HEADS].reshape(tokens_all, 1)
    inv2 = stat[:, HEADS + 1].reshape(tokens_all, 1)

    def norm_backward(upstream, normed, inv_std, gain):
        normed = normed.astype(F32)
        through = upstream * gain
        grad = inv_std * (
            through
            - jnp.mean(through, axis=-1, keepdims=True)
            - normed * jnp.mean(through * normed, axis=-1, keepdims=True)
        )
        return grad, jnp.sum(upstream * normed, axis=0), jnp.sum(upstream, axis=0)

    spread = jnp.zeros((batches, length, D), F32)
    pooled_grad = pooled_grad.reshape(batches, SLOTS, D)
    for number in range(SLOTS):
        spread = jnp.where(
            (seg[:, 0] == number)[:, :, None], pooled_grad[:, number][:, None, :], spread
        )
    grad_hidden = flat(cotangent[0].astype(F32) + spread)
    grad_h2, grad_gain2, grad_shift2 = norm_backward(
        grad_hidden, flat(normed2), inv2, gain_ffn.astype(F32)
    )
    d2 = grad_h2.astype(BF16)
    grad_w_outer = matmul_tn(flat(act), d2)
    grad_b_outer = jnp.sum(grad_h2, axis=0)
    grad_inner = matmul_nt(d2, w_outer) * flat(slope).astype(F32)
    d1 = grad_inner.astype(BF16)
    grad_w_inner = matmul_tn(flat(first_low), d1)
    grad_b_inner = jnp.sum(grad_inner, axis=0)
    grad_first = grad_h2 + matmul_nt(d1, w_inner)
    grad_h1, grad_gain1, grad_shift1 = norm_backward(
        grad_first, flat(normed1), inv1, gain_attn.astype(F32)
    )
    d0 = grad_h1.astype(BF16)
    grad_w_out = matmul_tn(flat(mixed), d0)
    grad_b_out = jnp.sum(grad_h1, axis=0)
    grad_mixed = matmul_nt(d0, w_out).astype(BF16).reshape(batches, length, D)
    dq, dk, dv, sums = attention_backward(q, k, v, grad_mixed, stat, seg)
    xf = flat(x)
    grad_w_query = matmul_tn(xf, flat(dq))
    grad_w_key = matmul_tn(xf, flat(dk))
    grad_w_value = matmul_tn(xf, flat(dv))
    sums = jnp.sum(sums, axis=0)
    token_grads = (
        grad_h1
        + matmul_nt(flat(dq), w_query)
        + matmul_nt(flat(dk), w_key)
        + matmul_nt(flat(dv), w_value)
    ).astype(BF16).reshape(1, batches, length, D)

    vectors = jnp.concatenate(
        [
            sums[0], sums[1], grad_b_out, grad_gain1, grad_shift1, grad_b_outer, grad_gain2,
            grad_shift2, grad_b_inner, jnp.zeros((4 * D,), F32),
        ]
    ).reshape(-1, D)
    total_outer = sum_over_devices(grad_w_outer, pairs, steps)
    total_inner = sum_over_devices(grad_w_inner, pairs, steps)
    total_attn, vectors = sum_over_devices(
        jnp.concatenate([grad_w_query, grad_w_key, grad_w_value, grad_w_out], axis=0),
        pairs, steps, vectors,
    )
    g_query, g_key, g_value, g_out = (total_attn[n * D : (n + 1) * D] for n in range(4))
    return (
        loss,
        unit.reshape(1, batches, SLOTS, D),
        unit_grad.reshape(1, batches, SLOTS, D),
        hidden[None],
        token_grads,
        g_query,
        vectors[0],
        g_key,
        g_value,
        vectors[1],
        g_out,
        vectors[2],
        vectors[3],
        vectors[4],
        total_inner,
        vectors[8 : 8 + ff // D].reshape(ff),
        total_outer,
        vectors[5],
        vectors[6],
        vectors[7],
    )


def solution(mesh):
    row = P("stream", None, "pairs", None)
    in_specs = (row, row, P(), row) + (P(),) * 15
    out_specs = (P("stream", None, "pairs"), row, row, row, row) + (P(),) * 15
    return jax.shard_map(
        on_device, mesh=mesh, in_specs=in_specs, out_specs=out_specs, check_vma=False
    )
```

```python
import functools
import jax
import jax.numpy as jnp
import numpy as np
from jax import lax
from jax.experimental import pallas as pl
from jax.experimental.pallas import tpu as pltpu
from jax.sharding import PartitionSpec as P

D = 768
HEADS = 12
HEAD_DIM = 64
SLOTS = 4
AXES = ("stream", "pairs")
F32 = jnp.float32
BF16 = jnp.bfloat16
HIGHEST = lax.Precision.HIGHEST
LOGIT_DIVISOR = 0.01
NORM_EPS = 1e-12
UNIT_EPS = 1e-06
NEG = -1000000000.0
SCALE = HEAD_DIM**-0.5
FF_CHUNK = 1536
MIB = 1 << 20
LONG = pl.CostEstimate(flops=1 << 44, bytes_accessed=1 << 38, transcendentals=0)

ORDER = (
    "gw1s", "B2", "gw1k", "B3", "at0", "gw2s", "0", "gw2k",
    "0", "at1", "0", "v", "1", "gw3s", "1", "gw3k",
    "0", "2", "0", "1", "2", "0", "1", "2",
    "1", "2", "1", "0", "2", "tok", "2", "1",
    "0", "2", "1", "2", "2",
)

TAIL_P = 0.305
TAIL = (
    0.12163973223592059,
    0.12246682364852957,
    0.10342082369335875,
    0.12102182071723708,
    -0.03797709812500149,
    0.18571719569775694,
    -0.15298848174013205,
    0.0366992308655468,
)


def dims(lhs, rhs, contract, **kw):
    return lax.dot_general(lhs, rhs, (contract, ((), ())), preferred_element_type=F32, **kw)


def matmul(lhs, rhs):
    return dims(lhs, rhs, ((1,), (0,)))


def matmul_nt(lhs, rhs):
    return dims(lhs, rhs, ((1,), (1,)))


def matmul_tn(lhs, rhs):
    return dims(lhs, rhs, ((0,), (0,)))


def norm_forward(total):
    centered = total - jnp.mean(total, axis=-1, keepdims=True)
    inv_std = lax.rsqrt(jnp.mean(centered * centered, axis=-1, keepdims=True) + NORM_EPS)
    return centered * inv_std, inv_std


def gelu_both(x):
    tail = 1.0 / (1.0 + TAIL_P * jnp.abs(x))
    poly = jnp.full_like(x, TAIL[-1])
    for coefficient in TAIL[-2::-1]:
        poly = poly * tail + coefficient
    bell = jnp.exp(-0.5 * (x * x))
    lower = poly * tail * bell
    phi = jnp.where(x >= 0, 1.0 - lower, lower)
    return x * phi, phi + x * bell * 0.3989422804014327


def segment_mask(seg_row):
    length = seg_row.shape[1]
    rows = jnp.broadcast_to(seg_row.astype(F32), (128, length))
    columns = rows.T
    wide = jnp.concatenate([columns] * (length // 128), axis=1)
    return jnp.where(wide == jnp.broadcast_to(seg_row.astype(F32), (length, length)), 0.0, NEG)


def forward_kernel(*refs):
    tokens, seg, wq, wk, wv, wo, wi_hbm, wo2_hbm = refs[:8]
    singles = refs[8:17]
    (
        q_out, k_out, v_out, mixed_out, stat_out, first_out, normed1_out, act_out, slope_out,
        normed2_out, hidden_out, pooled_out, unit_out, vectors, wi, wo2, mask, first_f32, acc, sem,
    ) = refs[17:]
    copy_in = pltpu.make_async_copy(wi_hbm, wi, sem.at[0])
    copy_out = pltpu.make_async_copy(wo2_hbm, wo2, sem.at[1])

    @pl.when(pl.program_id(0) == 0)
    def _():
        copy_in.start()
        copy_out.start()
        for row, single in enumerate(singles):
            for n in range(single.shape[0] // D):
                vectors[row + n : row + n + 1] = (
                    single[n * D : (n + 1) * D].astype(F32).reshape(1, D)
                )

    x = tokens[...]
    length = x.shape[0]
    q_out[...] = (matmul(x, wq[...]) + vectors[0:1]).astype(BF16)
    k_out[...] = matmul(x, wk[...]).astype(BF16)
    v_out[...] = (matmul(x, wv[...]) + vectors[1:2]).astype(BF16)
    mask[...] = segment_mask(seg[...])
    low_half = lax.broadcasted_iota(jnp.int32, (length, 128), 1) < HEAD_DIM

    def head_pair(pair, carry):
        lanes = pl.ds(pl.multiple_of(pair * 128, 128), 128)
        q2 = q_out[:, lanes] * BF16(SCALE)
        k2 = k_out[:, lanes]
        v2 = v_out[:, lanes].astype(F32).T.astype(BF16)
        outs = []
        for h in range(2):
            kh = jnp.where(low_half if h == 0 else ~low_half, k2, BF16(0))
            s = matmul_nt(kh, q2) + mask[...]
            top = jnp.max(s, axis=0, keepdims=True)
            e = jnp.exp(s - top)
            total = jnp.sum(e, axis=0, keepdims=True)
            o = matmul(v2[h * HEAD_DIM : (h + 1) * HEAD_DIM], e.astype(BF16)) * (1.0 / total)
            outs.append(o)
            stat_out[pl.ds(pair * 2 + h, 1), :] = top + jnp.log(total)
        mixed_out[:, lanes] = jnp.concatenate(outs, axis=0).T.astype(BF16)
        return carry

    lax.fori_loop(0, HEADS // 2, head_pair, 0, unroll=3)
    total = x.astype(F32) + (matmul(mixed_out[...], wo[...]) + vectors[2:3])
    normed1, inv1 = norm_forward(total)
    normed1_out[...] = normed1.astype(normed1_out.dtype)
    first = normed1 * vectors[3:4] + vectors[4:5]
    first_f32[...] = first
    first_out[...] = first.astype(BF16)

    @pl.when(pl.program_id(0) == 0)
    def _():
        copy_in.wait()
        copy_out.wait()

    acc[...] = jnp.zeros_like(acc)
    for chunk in range(wi.shape[1] // FF_CHUNK):
        lanes = pl.ds(chunk * FF_CHUNK, FF_CHUNK)
        row = 8 + chunk * (FF_CHUNK // D)
        shift = jnp.concatenate([vectors[row + n : row + n + 1] for n in range(FF_CHUNK // D)], axis=1)
        inner = matmul(first_out[...], wi[:, lanes]) + shift
        act, slope = gelu_both(inner)
        act = act.astype(BF16)
        act_out[:, lanes] = act
        slope_out[:, lanes] = slope.astype(slope_out.dtype)
        acc[...] += matmul(act, wo2[lanes, :])

    normed2, inv2 = norm_forward(first_f32[...] + (acc[...] + vectors[5:6]))
    normed2_out[...] = normed2.astype(normed2_out.dtype)
    hidden = normed2 * vectors[6:7] + vectors[7:8]
    hidden_out[...] = hidden.astype(BF16)
    slots = lax.broadcasted_iota(jnp.int32, (8, length), 0)
    one_hot = jnp.where(jnp.broadcast_to(seg[...], (8, length)) == slots, 1.0, 0.0)
    counted = jnp.maximum(jnp.sum(one_hot, axis=1, keepdims=True), 1.0)
    pooled = dims(one_hot, hidden, ((1,), (0,)), precision=HIGHEST) / counted
    pooled = pooled[:SLOTS]
    unit = (
        pooled * lax.rsqrt(jnp.mean(pooled * pooled, axis=-1, keepdims=True) + UNIT_EPS) * D**-0.5
    )
    for batch in range(pooled_out.shape[0] // SLOTS):

        @pl.when(pl.program_id(0) == batch)
        def _(batch=batch):
            pooled_out[batch * SLOTS : (batch + 1) * SLOTS] = pooled
            unit_out[batch * SLOTS : (batch + 1) * SLOTS] = unit

    stat_out[pl.ds(HEADS, 1), :] = jnp.broadcast_to(inv1, (length, 128)).T[:1]
    stat_out[pl.ds(HEADS + 1, 1), :] = jnp.broadcast_to(inv2, (length, 128)).T[:1]


def forward(tokens, segments, singles, w):
    batches, length, _ = tokens.shape
    ff = w["inner"].shape[1]

    def per_batch(rows, cols):
        return pl.BlockSpec((None, rows, cols), lambda b: (b, 0, 0))

    def whole(a):
        return pl.BlockSpec(a.shape, lambda b: (0,) * a.ndim, pipeline_mode=pl.Buffered(1))

    hbm = pl.BlockSpec(memory_space=pl.ANY)
    small = [w["query"], w["key"], w["value"], w["out"]]
    outs = [
        (length, D, BF16), (length, D, BF16), (length, D, BF16), (length, D, BF16),
        (16, length, F32), (length, D, BF16), (length, D, BF16), (length, ff, BF16),
        (length, ff, BF16), (length, D, BF16), (length, D, BF16),
    ]
    slot_rows = (batches * SLOTS, D)
    slot_spec = pl.BlockSpec(slot_rows, lambda b: (0, 0))
    return pl.pallas_call(
        forward_kernel,
        grid=(batches,),
        in_specs=[per_batch(length, D), per_batch(1, length)]
        + [whole(a) for a in small]
        + [hbm, hbm]
        + [whole(a) for a in singles],
        out_specs=[per_batch(r, c) for r, c, _ in outs] + [slot_spec] * 2 + [pl.BlockSpec((16, D), lambda b: (0, 0))],
        out_shape=[jax.ShapeDtypeStruct((batches, r, c), t) for r, c, t in outs]
        + [jax.ShapeDtypeStruct(slot_rows, F32)] * 2
        + [jax.ShapeDtypeStruct((16, D), F32)],
        scratch_shapes=[
            pltpu.VMEM((D, ff), BF16),
            pltpu.VMEM((ff, D), BF16),
            pltpu.VMEM((length, length), F32),
            pltpu.VMEM((length, D), F32),
            pltpu.VMEM((length, D), F32),
            pltpu.SemaphoreType.DMA((2,)),
        ],
        cost_estimate=LONG,
        compiler_params=pltpu.CompilerParams(vmem_limit_bytes=60 * MIB),
        name="forward_layer",
    )(tokens, segments, *small, w["inner"], w["outer"], *singles)


def attention_backward_kernel(q, k, v, do, stat, seg, *rest):
    dq_out, dk_out, dv_out, sums_out, mask = rest[-5:]
    length = q.shape[0]
    mask[...] = segment_mask(seg[...])
    low_half = lax.broadcasted_iota(jnp.int32, (length, 128), 1) < HEAD_DIM

    def head_pair(pair, carry):
        lanes = pl.ds(pl.multiple_of(pair * 128, 128), 128)
        q2 = q[:, lanes] * BF16(SCALE)
        k2 = k[:, lanes]
        v2 = v[:, lanes]
        do2 = do[:, lanes]
        k2t = (k2.astype(F32) * SCALE).T.astype(BF16)
        dqs, dks, dvs = [], [], []
        for h in range(2):
            half = low_half if h == 0 else ~low_half
            s = matmul_nt(jnp.where(half, k2, BF16(0)), q2) + mask[...]
            p = jnp.exp(s - stat[pl.ds(pair * 2 + h, 1), :])
            dp = matmul_nt(jnp.where(half, v2, BF16(0)), do2)
            pdp = p * dp
            delta = jnp.sum(pdp, axis=0, keepdims=True)
            ds = (pdp - p * delta).astype(BF16)
            dvs.append(matmul(p.astype(BF16), do2))
            dks.append(matmul(ds, q2))
            dqs.append(matmul(k2t[h * HEAD_DIM : (h + 1) * HEAD_DIM], ds))
        dq = jnp.concatenate(dqs, axis=0).T
        dk = jnp.where(low_half, dks[0], dks[1])
        dv = jnp.where(low_half, dvs[0], dvs[1])
        dq_out[:, lanes] = dq.astype(BF16)
        dk_out[:, lanes] = dk.astype(BF16)
        dv_out[:, lanes] = dv.astype(BF16)
        sums_out[0:1, lanes] = jnp.sum(dq, axis=0, keepdims=True)
        sums_out[1:2, lanes] = jnp.sum(dv, axis=0, keepdims=True)
        return carry

    lax.fori_loop(0, HEADS // 2, head_pair, 0)


def attention_backward(q, k, v, do, stat, segments, batch, into):
    batches, length, _ = q.shape

    def per_batch(rows, cols):
        return pl.BlockSpec((None, rows, cols), lambda i: (batch, 0, 0))

    wide = per_batch(length, D)
    shape = jax.ShapeDtypeStruct(q.shape, BF16)
    kept = pl.BlockSpec(memory_space=pl.ANY)
    return pl.pallas_call(
        attention_backward_kernel,
        grid=(1,),
        in_specs=[wide, wide, wide, wide, per_batch(16, length), per_batch(1, length)]
        + [kept] * len(into),
        out_specs=[wide, wide, wide, per_batch(8, D)],
        out_shape=[shape, shape, shape, jax.ShapeDtypeStruct((batches, 8, D), F32)],
        scratch_shapes=[pltpu.VMEM((length, length), F32)],
        input_output_aliases={6 + n: n for n in range(len(into))},
        cost_estimate=LONG,
        compiler_params=pltpu.CompilerParams(vmem_limit_bytes=48 * MIB),
        name="attention_backward",
    )(q, k, v, do, stat, segments, *into)


def first_backward_kernel(
    h2, d1, normed1, stat, vectors, w_inner, w_out, h1_out, d0_out, dm_out, sums_out
):
    length = h2.shape[0]
    upstream = h2[...] + matmul_nt(d1[...], w_inner[...])
    inv_std = jnp.broadcast_to(stat[HEADS : HEADS + 1, :], (128, length)).T[:, :1]
    normed = normed1[...].astype(F32)
    through = upstream * vectors[3:4]
    grad = inv_std * (
        through
        - jnp.mean(through, axis=-1, keepdims=True)
        - normed * jnp.mean(through * normed, axis=-1, keepdims=True)
    )
    h1_out[...] = grad
    low = grad.astype(BF16)
    d0_out[...] = low
    dm_out[...] = matmul_nt(low, w_out[...]).astype(BF16)

    @pl.when(pl.program_id(1) == 0)
    def _():
        sums_out[...] = jnp.zeros_like(sums_out)

    sums_out[0:1] += jnp.sum(grad, axis=0, keepdims=True)
    sums_out[1:2] += jnp.sum(upstream * normed, axis=0, keepdims=True)
    sums_out[2:3] += jnp.sum(upstream, axis=0, keepdims=True)


def first_backward(h2, d1, normed1, stat, vectors, w_inner, w_out):
    batches, length, _ = h2.shape
    ff = d1.shape[2]
    block = 512

    def rows(cols):
        return pl.BlockSpec((None, block, cols), lambda b, i: (b, i, 0))

    def whole(a):
        return pl.BlockSpec(a.shape, lambda b, i: (0, 0), pipeline_mode=pl.Buffered(1))

    return pl.pallas_call(
        first_backward_kernel,
        grid=(batches, length // block),
        in_specs=[
            rows(D), rows(ff), rows(D), pl.BlockSpec((None, 16, block), lambda b, i: (b, 0, i)),
            whole(vectors), whole(w_inner), whole(w_out),
        ],
        out_specs=[rows(D), rows(D), rows(D), pl.BlockSpec((None, 8, D), lambda b, i: (b, 0, 0))],
        out_shape=[
            jax.ShapeDtypeStruct(h2.shape, F32),
            jax.ShapeDtypeStruct(h2.shape, BF16),
            jax.ShapeDtypeStruct(h2.shape, BF16),
            jax.ShapeDtypeStruct((batches, 8, D), F32),
        ],
        cost_estimate=LONG,
        compiler_params=pltpu.CompilerParams(vmem_limit_bytes=48 * MIB),
        name="first_backward",
    )(h2, d1, normed1, stat, vectors, w_inner, w_out)


def pack_vectors(sums0, sums1, sums2, b_inner, rows):
    def kernel(attn, first, second, inner, out):
        out[...] = jnp.zeros_like(out)
        attn_sum = attn[0] + attn[1]
        first_sum = first[0] + first[1]
        second_sum = second[0] + second[1]
        out[0:2] = attn_sum[0:2]
        out[2:5] = first_sum[0:3]
        out[5:8] = second_sum[0:3]
        for n in range(inner.shape[1] // D):
            out[8 + n : 9 + n] = inner[:, n * D : (n + 1) * D]

    return pl.pallas_call(
        kernel, out_shape=jax.ShapeDtypeStruct((rows, D), F32), name="pack_vectors",
    )(sums0, sums1, sums2, b_inner)


def contrast_kernel(
    order, pairs_bits, counts, every, own, pooled, seg, loss_out, grad_out, pooled_grad_out
):
    rows = every.shape[0]
    everything = every[...]
    mine = own[...]
    me = lax.axis_index("pairs")
    my_stream = lax.axis_index("stream")
    my_core = me & 1

    def where_from(block):
        bit = {name: (block >> at) & 1 for at, name in enumerate(order)}
        core = my_core ^ bit["core"]
        straight = core == 0
        pair = me ^ bit["core"] ^ (jnp.where(straight, bit["xy"], bit["yx"]) << 1)
        for n in range(2, pairs_bits):
            pair = pair ^ (bit[n] << n)
        return my_stream ^ jnp.where(straight, bit["yx"], bit["xy"]), pair

    def batch_of(r):
        return (r >> 2) & 1

    r_col = lax.broadcasted_iota(jnp.int32, (rows, 1), 0)
    r_row = lax.broadcasted_iota(jnp.int32, (1, rows), 1)
    o_col = lax.broadcasted_iota(jnp.int32, (8, 1), 0)
    stream_col, pair_col = where_from(r_col >> 3)
    stream_row, pair_row = where_from(r_row >> 3)

    def count_step(p, carry):
        col, row = carry
        first, second = counts[0, p], counts[1, p]
        col = jnp.where(pair_col == p, jnp.where(batch_of(r_col) == 0, first, second), col)
        row = jnp.where(pair_row == p, jnp.where(batch_of(r_row) == 0, first, second), row)
        return col, row

    count_col, count_row = lax.fori_loop(
        0, 1 << pairs_bits, count_step, (jnp.zeros_like(r_col), jnp.zeros_like(r_row))
    )
    ok_col = (r_col & 3) < count_col
    ok_row = (r_row & 3) < count_row
    my_count = jnp.where(batch_of(o_col) == 0, counts[0, me], counts[1, me])
    my_ok = (o_col & 3) < my_count
    my_valid = my_ok.astype(F32)

    logits = dims(everything, everything, ((1,), (1,)), precision=HIGHEST) / LOGIT_DIVISOR
    related = (batch_of(r_col) == batch_of(r_row)) & (stream_col != stream_row) & ok_col
    masked = jnp.where(related, logits, NEG)
    top = jnp.max(masked, axis=0, keepdims=True)
    lse_row = top + jnp.log(jnp.sum(jnp.exp(masked - top), axis=0, keepdims=True))

    own_logits = dims(mine, everything, ((1,), (1,)), precision=HIGHEST) / LOGIT_DIVISOR
    other = (batch_of(o_col) == batch_of(r_row)) & (stream_row != my_stream)
    target = jnp.where(other & (pair_row == me) & ((o_col & 3) == (r_row & 3)), 1.0, 0.0)
    forward_logits = jnp.where(other & ok_row, own_logits, NEG)
    own_top = jnp.max(forward_logits, axis=1, keepdims=True)
    own_lse = own_top + jnp.log(
        jnp.sum(jnp.exp(forward_logits - own_top), axis=1, keepdims=True)
    )
    loss = (own_lse - jnp.sum(target * own_logits, axis=1, keepdims=True)) * my_valid
    loss_out[...] = jnp.broadcast_to(loss, loss_out.shape)
    forward_grad = (jnp.exp(forward_logits - own_lse) - target) * my_valid
    back_logits = jnp.where(other & my_ok, own_logits, NEG)
    back_grad = jnp.where(other & ok_row, jnp.exp(back_logits - lse_row) - target, 0.0)
    both = (forward_grad + back_grad) / LOGIT_DIVISOR
    grad = dims(both, everything, ((1,), (0,)), precision=HIGHEST)
    grad_out[...] = grad
    length = seg.shape[2]
    wide = (8, length)
    seg_rows = jnp.where(
        lax.broadcasted_iota(jnp.int32, wide, 0) < SLOTS,
        jnp.broadcast_to(seg[0], wide),
        jnp.broadcast_to(seg[1], wide),
    )
    in_slot = seg_rows == (lax.broadcasted_iota(jnp.int32, wide, 0) & 3)
    counted = jnp.sum(jnp.where(in_slot, 1.0, 0.0), axis=1, keepdims=True)
    pool = pooled[...]
    inv = lax.rsqrt(jnp.mean(pool * pool, axis=-1, keepdims=True) + UNIT_EPS)
    through = grad * D**-0.5
    inner = jnp.mean(pool * through, axis=-1, keepdims=True)
    pooled_grad_out[...] = (through * inv - pool * (inner * inv * inv * inv)) / counted


def contrast(order, pairs_bits, counts, every, own, pooled, seg):
    smem = pl.BlockSpec(memory_space=pltpu.SMEM)
    vmem = pl.BlockSpec(memory_space=pltpu.VMEM)
    return pl.pallas_call(
        functools.partial(contrast_kernel, order, pairs_bits),
        in_specs=[smem] + [vmem] * 4,
        out_specs=[vmem] * 3,
        out_shape=[
            jax.ShapeDtypeStruct((8, 128), F32),
            jax.ShapeDtypeStruct((8, D), F32),
            jax.ShapeDtypeStruct((8, D), F32),
        ],
        cost_estimate=LONG,
        compiler_params=pltpu.CompilerParams(vmem_limit_bytes=40 * MIB),
        name="contrast",
    )(counts, every, own, pooled, seg)


def norm2_backward_kernel(cot, normed2, stat, seg, pooled_grad, vectors, d2_out, grad_out, sums_out):
    length = cot.shape[0]
    batch = pl.program_id(0)
    columns = jnp.broadcast_to(stat[HEADS + 1 : HEADS + 2, :], (128, length)).T
    inv_std = columns[:, :1]
    seg_col = jnp.broadcast_to(seg[...].astype(F32), (128, length)).T[:, :1]
    spread = jnp.zeros((length, D), F32)
    for number in range(SLOTS):
        row = pooled_grad[pl.ds(batch * SLOTS + number, 1), :]
        spread = jnp.where(seg_col == float(number), row, spread)
    upstream = cot[...].astype(F32) + spread
    normed = normed2[...].astype(F32)
    through = upstream * vectors[6:7]
    grad = inv_std * (
        through
        - jnp.mean(through, axis=-1, keepdims=True)
        - normed * jnp.mean(through * normed, axis=-1, keepdims=True)
    )
    grad_out[...] = grad
    d2_out[...] = grad.astype(BF16)
    sums_out[0:1, :] = jnp.sum(grad, axis=0, keepdims=True)
    sums_out[1:2, :] = jnp.sum(upstream * normed, axis=0, keepdims=True)
    sums_out[2:3, :] = jnp.sum(upstream, axis=0, keepdims=True)


def norm2_backward(cot, normed2, stat, seg, pooled_grad, vectors):
    batches, length, _ = cot.shape

    def per_batch(rows, cols):
        return pl.BlockSpec((None, rows, cols), lambda b: (b, 0, 0))

    wide = per_batch(length, D)
    return pl.pallas_call(
        norm2_backward_kernel,
        grid=(batches,),
        in_specs=[
            wide, wide, per_batch(16, length), per_batch(1, length),
            pl.BlockSpec((8, D), lambda b: (0, 0)), pl.BlockSpec((16, D), lambda b: (0, 0)),
        ],
        out_specs=[wide, wide, per_batch(8, D)],
        out_shape=[
            jax.ShapeDtypeStruct(cot.shape, BF16),
            jax.ShapeDtypeStruct(cot.shape, F32),
            jax.ShapeDtypeStruct((batches, 8, D), F32),
        ],
        cost_estimate=LONG,
        compiler_params=pltpu.CompilerParams(vmem_limit_bytes=40 * MIB),
        name="norm2_backward",
    )(cot, normed2, stat, seg, pooled_grad, vectors)


def stages(pairs):
    bits = pairs.bit_length() - 1
    p = lax.axis_index("pairs")
    s = lax.axis_index("stream")
    core = p & 1

    def table(move):
        return [
            (a * pairs + b, move(a, b)[0] * pairs + move(a, b)[1])
            for a in range(2)
            for b in range(pairs)
        ]

    made = {
        "core": (core, table(lambda a, b: (a, b ^ 1))),
        "xy": (
            jnp.where(core == 0, (p >> 1) & 1, s),
            table(lambda a, b: (a, b ^ 2) if b % 2 == 0 else (a ^ 1, b)),
        ),
        "yx": (
            jnp.where(core == 0, s, (p >> 1) & 1),
            table(lambda a, b: (a ^ 1, b) if b % 2 == 0 else (a, b ^ 2)),
        ),
    }
    for n in range(2, bits):
        made[n] = ((p >> n) & 1, table(lambda a, b, n=n: (a, b ^ (1 << n))))
    return made


def send(value, permutation):
    return lax.ppermute(value, AXES, permutation)


def gather_all(value, steps, order):
    for name in order:
        value = jnp.concatenate([value, send(value, steps[name][1])], axis=0)
    return value


def kernel_call(kernel, grid, in_specs, out_specs, out_shape, name, scratch=(), limit=48):
    return pl.pallas_call(
        kernel,
        grid_spec=pltpu.PrefetchScalarGridSpec(
            num_scalar_prefetch=1, grid=grid, in_specs=in_specs, out_specs=out_specs,
            scratch_shapes=scratch,
        ),
        out_shape=out_shape,
        cost_estimate=LONG,
        compiler_params=pltpu.CompilerParams(vmem_limit_bytes=limit * MIB),
        name=name,
    )


def block_rows(rows, columns):
    block = rows
    while block * columns * 4 > 3 * MIB and block % 16 == 0:
        block //= 2
    return block


def split_sum(x, y, bit):
    rows, columns = x.shape
    half = rows // 2
    block = block_rows(half, columns)
    n = half // block

    def kernel(b, xs, ys, xk, yk, give, keep):
        give[...] = xs[...] + ys[...]
        keep[...] = xk[...] + yk[...]

    other = pl.BlockSpec((block, columns), lambda i, b: ((1 - b[0]) * n + i, 0))
    own = pl.BlockSpec((block, columns), lambda i, b: (b[0] * n + i, 0))
    out = pl.BlockSpec((block, columns), lambda i, b: (i, 0))
    shape = jax.ShapeDtypeStruct((half, columns), F32)
    return kernel_call(
        kernel, (n,), [other, other, own, own], [out, out], [shape, shape], "split_sum"
    )(bit, x, y, x, y)


def join(own, got, bit):
    rows, columns = own.shape
    block = block_rows(rows, columns)
    n = rows // block

    def kernel(b, mine, other, out):
        @pl.when(pl.program_id(0) == 0)
        def _():
            out[...] = mine[...]

        @pl.when(pl.program_id(0) != 0)
        def _():
            out[...] = other[...]

    return kernel_call(
        kernel, (2, n),
        [
            pl.BlockSpec((block, columns), lambda j, i, b: (jnp.where(j == 0, i, n - 1), 0)),
            pl.BlockSpec((block, columns), lambda j, i, b: (jnp.where(j == 0, 0, i), 0)),
        ],
        pl.BlockSpec((block, columns), lambda j, i, b: (jnp.where(j == 0, b[0], 1 - b[0]) * n + i, 0)),
        jax.ShapeDtypeStruct((2 * rows, columns), F32), "join",
    )(bit, own, got)


def rearrange(inputs, bits, outputs, pieces, name):
    def kernel(at, *refs):
        sources, targets = refs[: len(inputs)], refs[len(inputs) :]

        def place(row, choice, rows):
            if choice is None:
                return pl.ds(row, rows)
            bit = at[choice[0]] if not choice[1] else 1 - at[choice[0]]
            return pl.ds(pl.multiple_of(row + bit * rows, 8), rows)

        for target, row, choice, rows, terms in pieces:
            total = None
            for source, start, pick in terms:
                value = sources[source][place(start, pick, rows), :]
                total = value if total is None else total + value
            targets[target][place(row, choice, rows), :] = total

    def whole(rows):
        return pl.BlockSpec((rows, D), lambda i, at: (0, 0))

    return kernel_call(
        kernel, (1,), [whole(a.shape[0]) for a in inputs], [whole(rows) for rows in outputs],
        [jax.ShapeDtypeStruct((rows, D), F32) for rows in outputs], name,
    )(jnp.stack(bits).astype(jnp.int32), *inputs)


def split_attention(total, blocks):
    deep = 2 * D // 3
    return total - deep, deep


def join_attention(own, got, bit, blocks):
    rows = own.shape[0]
    wide, deep = split_attention(rows, blocks)
    per = wide // blocks
    step = per - 8
    cut = blocks * step - D

    def kernel(b, own, got, query, key, value, out, vectors):
        def write(half, source, first, second):
            for n in range(blocks):
                piece = source[n * per : n * per + step]
                if n * step < D:
                    first[n * step : (n + 1) * step] = piece
                else:
                    second[n * step - D : (n + 1) * step - D] = piece
                vectors[half * blocks + n : half * blocks + n + 1] = source[
                    n * per + step : n * per + step + 1
                ]
            second[cut:] = source[wide:]

        @pl.when(b[0] == 0)
        def _():
            write(0, own, query, key)
            write(1, got, value, out)

        @pl.when(b[0] != 0)
        def _():
            write(0, got, query, key)
            write(1, own, value, out)

    def whole(count):
        return pl.BlockSpec((count, D), lambda i, b: (0, 0))

    return kernel_call(
        kernel, (1,), [whole(rows)] * 2, [whole(D)] * 4 + [whole(2 * blocks)],
        [jax.ShapeDtypeStruct((D, D), F32)] * 4 + [jax.ShapeDtypeStruct((2 * blocks, D), F32)],
        "join_attention",
    )(bit, own, got)


def outer_grad_half(act, d2, half):
    tokens, ff = act.shape
    n = ff // 2 // D

    def kernel(b, left, right, out):
        out[...] = matmul_tn(left[...], right[...])

    return kernel_call(
        kernel, (n,),
        [pl.BlockSpec((tokens, D), lambda i, b: (0, b[0] * n + i)), pl.BlockSpec((tokens, D), lambda i, b: (0, 0))],
        pl.BlockSpec((D, D), lambda i, b: (i, 0)),
        jax.ShapeDtypeStruct((ff // 2, D), F32), "outer_grad",
    )(half, act, d2)


def inner_grad_half(first, d1, half):
    tokens, ff = d1.shape
    n = ff // 2 // D

    def kernel(b, left, right, out):
        out[...] = matmul_tn(left[...], right[...])

    return kernel_call(
        kernel, (n,),
        [pl.BlockSpec((tokens, D), lambda i, b: (0, 0)), pl.BlockSpec((tokens, D), lambda i, b: (0, b[0] * n + i))],
        pl.BlockSpec((D, D), lambda i, b: (i, 0)),
        jax.ShapeDtypeStruct((ff // 2, D), F32), "inner_grad",
    )(half, first, d1)


def grad_split(wide, left, right, got, which):
    tokens = left.shape[0]

    def kernel(b, left, right, got, give, keep):
        total = matmul_tn(left[...], right[...]) + got[...]

        @pl.when(pl.program_id(0) == 0)
        def _():
            give[...] = total

        @pl.when(pl.program_id(0) != 0)
        def _():
            keep[...] = total

    def pick(i, b):
        return jnp.where(i == 0, 1 - b[1], b[1])

    moving = pl.BlockSpec((tokens, D), lambda i, b: (0, b[0] * 2 + pick(i, b)))
    still = pl.BlockSpec((tokens, D), lambda i, b: (0, 0))
    block = pl.BlockSpec((D, D), lambda i, b: (0, 0))
    shape = jax.ShapeDtypeStruct((D, D), F32)
    return kernel_call(
        kernel, (2,),
        [moving if wide else still, still if wide else moving, pl.BlockSpec((D, D), lambda i, b: (pick(i, b), 0))],
        [block, block], [shape, shape], "grad_split",
    )(which, left, right, got)


def join_into(own, got, bits, across):
    rows, columns = own.shape
    block = block_rows(rows, columns)
    n = rows // block

    def kernel(b, mine, other, out, final):
        @pl.when(pl.program_id(0) == 0)
        def _():
            out[...] = mine[...]
            final[...] = mine[...]

        @pl.when(pl.program_id(0) != 0)
        def _():
            out[...] = other[...]
            final[...] = other[...]

    def at(j, i, b):
        return jnp.where(j == 0, b[0], 1 - b[0]) * n + i

    per = D // block

    def final_at(j, i, b):
        row = b[1] * 2 * n + at(j, i, b)
        return (row % per, row // per) if across else (row, 0)

    shape = (D, 4 * rows // D * D) if across else (4 * rows, columns)
    return kernel_call(
        kernel, (2, n),
        [
            pl.BlockSpec((block, columns), lambda j, i, b: (jnp.where(j == 0, i, n - 1), 0)),
            pl.BlockSpec((block, columns), lambda j, i, b: (jnp.where(j == 0, 0, i), 0)),
        ],
        [
            pl.BlockSpec((block, columns), lambda j, i, b: (at(j, i, b), 0)),
            pl.BlockSpec((block, columns), final_at),
        ],
        [jax.ShapeDtypeStruct((2 * rows, columns), F32), jax.ShapeDtypeStruct(shape, F32)], "join_into",
    )(bits, own, got)


def place(got, final, bit, across):
    rows, columns = got.shape
    block = block_rows(D, columns)
    n = rows // block
    per = D // block

    def kernel(b, other, _, out):
        out[...] = other[...]

    def at(i, b):
        row = (1 - b[0]) * n + i
        return (row % per, row // per) if across else (row, 0)

    return pl.pallas_call(
        kernel,
        grid_spec=pltpu.PrefetchScalarGridSpec(
            num_scalar_prefetch=1, grid=(n,),
            in_specs=[
                pl.BlockSpec((block, columns), lambda i, b: (i, 0)), pl.BlockSpec(memory_space=pl.ANY)
            ],
            out_specs=pl.BlockSpec((block, columns), at),
        ),
        out_shape=jax.ShapeDtypeStruct(final.shape, F32),
        input_output_aliases={2: 0},
        cost_estimate=LONG,
        compiler_params=pltpu.CompilerParams(vmem_limit_bytes=48 * MIB),
        name="place",
    )(bit, got, final)


def attention_grad_half(x, mixed, dq, dk, dv, d0, vectors, half):
    tokens = x.shape[0]
    blocks = vectors.shape[0] // 2
    cut = 4 * D // 3 - D
    step = (D + cut) // blocks
    per = step + 8

    wide = blocks * per

    def kernel(b, x, mixed, dq, dk, dv, d0, vectors, out):
        def write(first, second, base):
            for n in range(blocks):
                start = n * step
                piece = first[start : start + step] if start < D else second[start - D : start - D + step]
                out[n * per : n * per + step] = piece
                out[n * per + step : (n + 1) * per] = jnp.broadcast_to(
                    vectors[base + n : base + n + 1], (8, D)
                )
            out[wide:] = second[cut:]

        @pl.when(b[0] == 0)
        def _():
            write(matmul_tn(x[...], dq[...]), matmul_tn(x[...], dk[...]), 0)

        @pl.when(b[0] != 0)
        def _():
            write(matmul_tn(x[...], dv[...]), matmul_tn(mixed[...], d0[...]), blocks)

    def whole(rows):
        return pl.BlockSpec((rows, D), lambda i, b: (0, 0))

    return kernel_call(
        kernel, (1,), [whole(tokens)] * 6 + [whole(2 * blocks)], whole(wide + D - cut),
        jax.ShapeDtypeStruct((wide + D - cut, D), F32),
        "attention_grad",
    )(half, x, mixed, dq, dk, dv, d0, vectors)


class Line:
    def __init__(self, **start):
        self.at = dict(start)
        self.last = []

    def step(self, function, given, made):
        names = list(dict.fromkeys(list(given) + self.last))
        held = lax.optimization_barrier([self.at[name] for name in names])
        self.at.update(zip(names, held))
        got = function(*[self.at[name] for name in given])
        self.at.update(zip(made, got))
        self.last = list(made)


class Sum:
    def __init__(self, line, name, steps, route, last, across, result):
        self.line, self.name, self.steps = line, name, steps
        self.route, self.swap, self.across, self.result = route, last, across, result
        self.visits = 0

    def bit(self, step):
        return self.steps[step][0].reshape(1).astype(jnp.int32)

    def start(self, give):
        self.line.at[self.name + ".got"] = send(give, self.steps[self.route[0]][1])

    def visit(self):
        line, route = self.line, self.route
        keep, got = self.name + ".keep", self.name + ".got"
        n, at = len(route), self.visits
        self.visits += 1
        if at < n - 1:
            bit = self.bit(route[at + 1])
            line.step(lambda k, g: split_sum(k, g, bit), [keep, got], [self.name + ".give", keep])
            self.line.at[got] = send(self.line.at[self.name + ".give"], self.steps[route[at + 1]][1])
        elif at <= n:
            line.step(lambda k, g: (k + g,), [keep, got], [keep])
            step = self.swap if at == n - 1 else route[n - 1]
            self.line.at[got] = send(self.line.at[keep], self.steps[step][1])
        elif at < 2 * n:
            step = route[2 * n - at]
            bit = self.bit(step)
            if at == 2 * n - 1:
                bits = jnp.concatenate([bit, self.bit(route[0])])
                line.step(
                    lambda k, g: join_into(k, g, bits, self.across), [keep, got], [keep, self.name + ".all"]
                )
            else:
                line.step(lambda k, g: (join(k, g, bit),), [keep, got], [keep])
            self.line.at[got] = send(self.line.at[keep], self.steps[route[2 * n - at - 1]][1])
        else:
            bit = self.bit(route[0])
            line.step(
                lambda g, final: (place(g, final, bit, self.across),), [got, self.name + ".all"], [self.result]
            )

    def keep_and_split(self, wide, given):
        self.visits = 1
        which = jnp.concatenate([self.bit(self.route[0]), self.bit(self.route[1])])
        made = [self.name + ".give", self.name + ".keep"]
        self.line.step(
            lambda a, b, got: grad_split(wide, a, b, got, which), given + [self.name + ".got"], made
        )
        self.line.at[self.name + ".got"] = send(self.line.at[made[0]], self.steps[self.route[1]][1])


class PairSum:
    def __init__(self, line, name, steps, routes, last, finish, results):
        self.line, self.name, self.steps = line, name, steps
        self.routes, self.swap, self.finish, self.results = routes, last, finish, results
        self.visits = 0
        self.names = []

    def start(self, give, rows):
        self.rows = list(rows)
        self.line.at[self.name + ".got0"] = send(give, self.steps["core"][1])
        self.got = [(self.name + ".got0", 0), (self.name + ".got0", rows[0])]
        self.keep = [(self.name + ".keep", 0), (self.name + ".keep", rows[0])]

    def plan(self, step_names, rows):
        if step_names[0] == step_names[1]:
            return [(0, 0), (0, rows[0])], [rows[0] + rows[1]], [step_names[0]]
        return [(0, 0), (1, 0)], list(rows), list(step_names)

    def go(self, pieces_of, out_rows, sends, made):
        names = []
        for part in self.keep + self.got:
            if part[0] not in names:
                names.append(part[0])
        pieces, bits = pieces_of(names)
        if not bits:
            bits = [self.steps["core"][0]]
        self.line.step(
            lambda *a: rearrange(a, bits, out_rows, pieces, "rearrange"), names, made
        )
        for name, step, got in sends:
            self.line.at[got] = send(self.line.at[name], self.steps[step][1])

    def visit(self):
        line, n, at = self.line, len(self.routes[0]), self.visits
        tag = f"{self.name}.{at}."
        self.visits += 1
        if at == 2 * n:
            bit = self.steps["core"][0].reshape(1).astype(jnp.int32)
            line.step(
                lambda k, g: self.finish(k, g, bit), [self.keep[0][0], self.got[0][0]], self.results
            )
            return
        if at < n - 1:
            after = [route[at + 1] for route in self.routes]
            half = [rows // 2 for rows in self.rows]
            where, outs, steps = self.plan(after, half)
            made = [tag + f"give{i}" for i in range(len(outs))] + [tag + "keep0", tag + "keep1"]

            def pieces_of(names):
                pieces, bits = [], []
                for part in range(2):
                    bits.append(self.steps[after[part]][0])
                    for flip, (target, row) in ((True, where[part]), (False, (len(outs) + part, 0))):
                        terms = [
                            (names.index(source[part][0]), source[part][1], (part, flip))
                            for source in (self.keep, self.got)
                        ]
                        pieces.append((target, row, None, half[part], terms))
                return pieces, bits

            sends = [(made[i], steps[i], tag + f"got{i}") for i in range(len(outs))]
            self.go(pieces_of, outs + half, sends, made)
            self.rows = half
            self.keep = [(tag + "keep0", 0), (tag + "keep1", 0)]
            self.got = [(tag + f"got{where[part][0]}", where[part][1]) for part in range(2)]
            return
        if at <= n:
            after = [self.swap] * 2 if at == n - 1 else [route[n - 1] for route in self.routes]
            rows, grown = self.rows, self.rows
        else:
            back = [route[2 * n - at] for route in self.routes]
            after = [route[2 * n - at - 1] for route in self.routes]
            rows, grown = self.rows, [2 * r for r in self.rows]
        where, outs, steps = self.plan(after, grown)
        made = [tag + f"own{i}" for i in range(len(outs))]

        def pieces_of(names):
            pieces, bits = [], []
            for part in range(2):
                target, row = where[part]
                mine, other = (
                    (names.index(source[part][0]), source[part][1], None) for source in (self.keep, self.got)
                )
                if at <= n:
                    pieces.append((target, row, None, rows[part], [mine, other]))
                else:
                    bits.append(self.steps[back[part]][0])
                    pieces.append((target, row, (part, False), rows[part], [mine]))
                    pieces.append((target, row, (part, True), rows[part], [other]))
            return pieces, bits

        sends = [(made[i], steps[i], tag + f"got{i}") for i in range(len(outs))]
        self.go(pieces_of, outs, sends, made)
        self.rows = list(grown)
        self.keep = [(tag + f"own{where[part][0]}", where[part][1]) for part in range(2)]
        self.got = [(tag + f"got{where[part][0]}", where[part][1]) for part in range(2)]


def on_device(
    tokens, segments, counts, cotangent, w_query, b_query, w_key, w_value, b_value, w_out, b_out,
    gain_attn, bias_attn, w_inner, b_inner, w_outer, b_outer, gain_ffn, bias_ffn,
):
    pairs = lax.axis_size("pairs")
    bits = pairs.bit_length() - 1
    batches, length = tokens.shape[1], tokens.shape[2]
    ff = w_inner.shape[1]
    stream = lax.axis_index("stream")
    pair = lax.axis_index("pairs")
    steps = stages(pairs)
    w = dict(
        query=w_query, b_query=b_query, key=w_key, value=w_value, b_value=b_value, out=w_out,
        b_out=b_out, gain1=gain_attn, shift1=bias_attn, inner=w_inner, b_inner=b_inner,
        outer=w_outer, b_outer=b_outer, gain2=gain_ffn, shift2=bias_ffn,
    )
    x = tokens[0]
    seg = segments[0]
    order = list(range(bits - 1, 1, -1)) + ["xy", "yx", "core"]
    singles = [b_query, b_value, b_out, gain_attn, bias_attn, b_outer, gain_ffn, bias_ffn, b_inner]
    (
        q, k, v, mixed, stat, first_low, normed1, act, slope, normed2, hidden, pooled, unit, vectors
    ) = forward(x, seg, singles, w)
    every = gather_all(unit, steps, order)
    loss, unit_grad, pooled_grad = contrast(
        order, bits, counts, every, unit, pooled, seg
    )
    loss = loss[:, 0].reshape(1, batches, SLOTS)
    d2, grad_h2, sums2 = norm2_backward(cotangent[0], normed2, stat, seg, pooled_grad, vectors)

    tokens_all = batches * length
    flat = lambda a: a.reshape(tokens_all, a.shape[-1])
    core = steps["core"][0].reshape(1).astype(jnp.int32)
    line = Line(
        d2=flat(d2), act=flat(act), slope=flat(slope), h2=grad_h2, first=flat(first_low),
        normed1=normed1, q=q,
    )
    middle = list(range(3, bits - 1))
    flat_route = ["core", "xy", "yx", 2] + middle
    deep_route = ["core", 2, "yx", "xy"] + middle
    last = bits - 1
    blocks = 1 << len(flat_route)
    outer = Sum(line, "outer", steps, flat_route, last, False, "total_outer")
    inner = Sum(line, "inner", steps, flat_route, last, True, "total_inner")
    rest = PairSum(
        line, "rest", steps, (flat_route, deep_route), last,
        lambda k, g, b: join_attention(k, g, b, blocks // 2),
        ["total_query", "total_key", "total_value", "total_out", "vectors"],
    )
    xf, mixed_f = flat(x), flat(mixed)

    def give(group, function, given):
        name = group.name + ".give"
        line.step(lambda *a: (function(*a, 1 - core),), given, [name])
        if group is rest:
            group.start(line.at[name], split_attention(line.at[name].shape[0], blocks // 2))
        else:
            group.start(line.at[name])

    def keep(group, function, given):
        line.step(lambda *a: (function(*a, core),), given, [group.name + ".keep"])

    def inner_step(d2, slope):
        grad_inner = matmul_nt(d2, w_outer) * slope.astype(F32)
        return grad_inner.astype(BF16), jnp.sum(grad_inner, axis=0, keepdims=True)

    def first_step(d1, h2, normed):
        d1 = d1.reshape(batches, length, ff)
        h1, d0, dm, sums = first_backward(h2, d1, normed, stat, vectors, w_inner, w_out)
        return flat(h1), flat(d0), dm, sums

    def attention(batch):
        names = ["dq", "dk", "dv", "sums0"]
        into = names if batch else []
        line.step(
            lambda q, dm, *into: attention_backward(q, k, v, dm, stat, seg, batch, into),
            ["q", "dm"] + into, names,
        )

    def attention_grads(d0, dq, dk, dv, vectors, half):
        return attention_grad_half(xf, mixed_f, flat(dq), flat(dk), flat(dv), d0, vectors, half)

    attention_given = ["d0", "dq", "dk", "dv", "vec"]

    def token_gradient(h1, dq, dk, dv):
        return (
            (
                h1
                + matmul_nt(flat(dq), w_query)
                + matmul_nt(flat(dk), w_key)
                + matmul_nt(flat(dv), w_value)
            ).astype(BF16),
        )

    def vector_step():
        line.step(
            lambda a, b, c: (pack_vectors(a, b, sums2, c, blocks),), ["sums0", "sums1", "b_inner"], ["vec"]
        )

    actions = {
        "gw1s": lambda: give(outer, outer_grad_half, ["act", "d2"]),
        "gw1k": lambda: outer.keep_and_split(True, ["act", "d2"]),
        "B2": lambda: line.step(inner_step, ["d2", "slope"], ["d1", "b_inner"]),
        "gw2s": lambda: give(inner, inner_grad_half, ["first", "d1"]),
        "gw2k": lambda: inner.keep_and_split(False, ["first", "d1"]),
        "B3": lambda: line.step(first_step, ["d1", "h2", "normed1"], ["h1", "d0", "dm", "sums1"]),
        "at0": lambda: attention(0),
        "at1": lambda: attention(1),
        "gw3s": lambda: give(rest, attention_grads, attention_given),
        "gw3k": lambda: keep(rest, attention_grads, attention_given),
        "tok": lambda: line.step(token_gradient, ["h1", "dq", "dk", "dv"], ["tokens"]),
        "v": vector_step,
        "0": outer.visit,
        "1": inner.visit,
        "2": rest.visit,
    }
    for action in ORDER:
        actions[action]()
    for group in (inner, outer, rest):
        while group.visits < 2 * len(flat_route) + 1:
            group.visit()
    total = line.at
    sums = total["vectors"]
    return (
        loss,
        unit.reshape(1, batches, SLOTS, D),
        unit_grad.reshape(1, batches, SLOTS, D),
        hidden[None],
        total["tokens"].reshape(1, batches, length, D),
        total["total_query"],
        sums[0],
        total["total_key"],
        total["total_value"],
        sums[1],
        total["total_out"],
        sums[2],
        sums[3],
        sums[4],
        total["total_inner"],
        sums[8 : 8 + ff // D].reshape(ff),
        total["total_outer"],
        sums[5],
        sums[6],
        sums[7],
    )


def solution(mesh):
    row = P("stream", None, "pairs", None)
    in_specs = (row, row, P(), row) + (P(),) * 15
    out_specs = (P("stream", None, "pairs"), row, row, row, row) + (P(),) * 15
    return jax.shard_map(
        on_device, mesh=mesh, in_specs=in_specs, out_specs=out_specs, check_vma=False
    )
```

```python
import functools
import jax
import jax.numpy as jnp
import numpy as np
from jax import lax
from jax.experimental import pallas as pl
from jax.experimental.pallas import tpu as pltpu
from jax.sharding import PartitionSpec as P

D = 768
HEADS = 12
HEAD_DIM = 64
SLOTS = 4
AXES = ("stream", "pairs")
F32 = jnp.float32
BF16 = jnp.bfloat16
HIGHEST = lax.Precision.HIGHEST
LOGIT_DIVISOR = 0.01
NORM_EPS = 1e-12
UNIT_EPS = 1e-06
NEG = -1000000000.0
SCALE = HEAD_DIM**-0.5
FF_CHUNK = 1536
MIB = 1 << 20
LONG = pl.CostEstimate(flops=1 << 44, bytes_accessed=1 << 38, transcendentals=0)

ORDER = (
    "gw1s", "B2", "gw1k", "B3", "at0", "gw2s", "0", "gw2k",
    "0", "at1", "0", "v", "1", "gw3s", "1", "gw3k",
    "0", "2", "0", "1", "2", "0", "1", "2",
    "1", "2", "1", "0", "2", "tok", "2", "0",
    "1", "2", "2", "1", "2",
)

TAIL_P = 0.305
TAIL = (
    0.12163973223592059,
    0.12246682364852957,
    0.10342082369335875,
    0.12102182071723708,
    -0.03797709812500149,
    0.18571719569775694,
    -0.15298848174013205,
    0.0366992308655468,
)


def dims(lhs, rhs, contract, **kw):
    return lax.dot_general(lhs, rhs, (contract, ((), ())), preferred_element_type=F32, **kw)


def matmul(lhs, rhs):
    return dims(lhs, rhs, ((1,), (0,)))


def matmul_nt(lhs, rhs):
    return dims(lhs, rhs, ((1,), (1,)))


def matmul_tn(lhs, rhs):
    return dims(lhs, rhs, ((0,), (0,)))


def norm_forward(total):
    centered = total - jnp.mean(total, axis=-1, keepdims=True)
    inv_std = lax.rsqrt(jnp.mean(centered * centered, axis=-1, keepdims=True) + NORM_EPS)
    return centered * inv_std, inv_std


def gelu_both(x):
    tail = 1.0 / (1.0 + TAIL_P * jnp.abs(x))
    poly = jnp.full_like(x, TAIL[-1])
    for coefficient in TAIL[-2::-1]:
        poly = poly * tail + coefficient
    bell = jnp.exp(-0.5 * (x * x))
    lower = poly * tail * bell
    phi = jnp.where(x >= 0, 1.0 - lower, lower)
    return x * phi, phi + x * bell * 0.3989422804014327


def segment_mask(seg_row):
    length = seg_row.shape[1]
    rows = jnp.broadcast_to(seg_row.astype(F32), (128, length))
    columns = rows.T
    wide = jnp.concatenate([columns] * (length // 128), axis=1)
    return jnp.where(wide == jnp.broadcast_to(seg_row.astype(F32), (length, length)), 0.0, NEG)


def forward_kernel(*refs):
    tokens, seg, wq, wk, wv, wo, wi_hbm, wo2_hbm = refs[:8]
    singles = refs[8:17]
    (
        q_out, k_out, v_out, mixed_out, stat_out, first_out, normed1_out, act_out, slope_out,
        normed2_out, hidden_out, pooled_out, unit_out, vectors, wi, wo2, mask, first_f32, acc, sem,
    ) = refs[17:]
    copy_in = pltpu.make_async_copy(wi_hbm, wi, sem.at[0])
    copy_out = pltpu.make_async_copy(wo2_hbm, wo2, sem.at[1])

    @pl.when(pl.program_id(0) == 0)
    def _():
        copy_in.start()
        copy_out.start()
        for row, single in enumerate(singles):
            for n in range(single.shape[0] // D):
                vectors[row + n : row + n + 1] = (
                    single[n * D : (n + 1) * D].astype(F32).reshape(1, D)
                )

    x = tokens[...]
    length = x.shape[0]
    q_out[...] = (matmul(x, wq[...]) + vectors[0:1]).astype(BF16)
    k_out[...] = matmul(x, wk[...]).astype(BF16)
    v_out[...] = (matmul(x, wv[...]) + vectors[1:2]).astype(BF16)
    mask[...] = segment_mask(seg[...])
    low_half = lax.broadcasted_iota(jnp.int32, (length, 128), 1) < HEAD_DIM

    def head_pair(pair, carry):
        lanes = pl.ds(pl.multiple_of(pair * 128, 128), 128)
        q2 = q_out[:, lanes] * BF16(SCALE)
        k2 = k_out[:, lanes]
        v2 = v_out[:, lanes].astype(F32).T.astype(BF16)
        outs = []
        for h in range(2):
            kh = jnp.where(low_half if h == 0 else ~low_half, k2, BF16(0))
            s = matmul_nt(kh, q2) + mask[...]
            top = jnp.max(s, axis=0, keepdims=True)
            e = jnp.exp(s - top)
            total = jnp.sum(e, axis=0, keepdims=True)
            o = matmul(v2[h * HEAD_DIM : (h + 1) * HEAD_DIM], e.astype(BF16)) * (1.0 / total)
            outs.append(o)
            stat_out[pl.ds(pair * 2 + h, 1), :] = top + jnp.log(total)
        mixed_out[:, lanes] = jnp.concatenate(outs, axis=0).T.astype(BF16)
        return carry

    lax.fori_loop(0, HEADS // 2, head_pair, 0, unroll=3)
    total = x.astype(F32) + (matmul(mixed_out[...], wo[...]) + vectors[2:3])
    normed1, inv1 = norm_forward(total)
    normed1_out[...] = normed1.astype(normed1_out.dtype)
    first = normed1 * vectors[3:4] + vectors[4:5]
    first_f32[...] = first
    first_out[...] = first.astype(BF16)

    @pl.when(pl.program_id(0) == 0)
    def _():
        copy_in.wait()
        copy_out.wait()

    acc[...] = jnp.zeros_like(acc)
    for chunk in range(wi.shape[1] // FF_CHUNK):
        lanes = pl.ds(chunk * FF_CHUNK, FF_CHUNK)
        row = 8 + chunk * (FF_CHUNK // D)
        shift = jnp.concatenate([vectors[row + n : row + n + 1] for n in range(FF_CHUNK // D)], axis=1)
        inner = matmul(first_out[...], wi[:, lanes]) + shift
        act, slope = gelu_both(inner)
        act = act.astype(BF16)
        act_out[:, lanes] = act
        slope_out[:, lanes] = slope.astype(slope_out.dtype)
        acc[...] += matmul(act, wo2[lanes, :])

    normed2, inv2 = norm_forward(first_f32[...] + (acc[...] + vectors[5:6]))
    normed2_out[...] = normed2.astype(normed2_out.dtype)
    hidden = normed2 * vectors[6:7] + vectors[7:8]
    hidden_out[...] = hidden.astype(BF16)
    slots = lax.broadcasted_iota(jnp.int32, (8, length), 0)
    one_hot = jnp.where(jnp.broadcast_to(seg[...], (8, length)) == slots, 1.0, 0.0)
    counted = jnp.maximum(jnp.sum(one_hot, axis=1, keepdims=True), 1.0)
    pooled = dims(one_hot, hidden, ((1,), (0,)), precision=HIGHEST) / counted
    pooled = pooled[:SLOTS]
    unit = (
        pooled * lax.rsqrt(jnp.mean(pooled * pooled, axis=-1, keepdims=True) + UNIT_EPS) * D**-0.5
    )
    for batch in range(pooled_out.shape[0] // SLOTS):

        @pl.when(pl.program_id(0) == batch)
        def _(batch=batch):
            pooled_out[batch * SLOTS : (batch + 1) * SLOTS] = pooled
            unit_out[batch * SLOTS : (batch + 1) * SLOTS] = unit

    stat_out[pl.ds(HEADS, 1), :] = jnp.broadcast_to(inv1, (length, 128)).T[:1]
    stat_out[pl.ds(HEADS + 1, 1), :] = jnp.broadcast_to(inv2, (length, 128)).T[:1]


def forward(tokens, segments, singles, w):
    batches, length, _ = tokens.shape
    ff = w["inner"].shape[1]

    def per_batch(rows, cols):
        return pl.BlockSpec((None, rows, cols), lambda b: (b, 0, 0))

    def whole(a):
        return pl.BlockSpec(a.shape, lambda b: (0,) * a.ndim, pipeline_mode=pl.Buffered(1))

    hbm = pl.BlockSpec(memory_space=pl.ANY)
    small = [w["query"], w["key"], w["value"], w["out"]]
    outs = [
        (length, D, BF16), (length, D, BF16), (length, D, BF16), (length, D, BF16),
        (16, length, F32), (length, D, BF16), (length, D, BF16), (length, ff, BF16),
        (length, ff, BF16), (length, D, BF16), (length, D, BF16),
    ]
    slot_rows = (batches * SLOTS, D)
    slot_spec = pl.BlockSpec(slot_rows, lambda b: (0, 0))
    return pl.pallas_call(
        forward_kernel,
        grid=(batches,),
        in_specs=[per_batch(length, D), per_batch(1, length)]
        + [whole(a) for a in small]
        + [hbm, hbm]
        + [whole(a) for a in singles],
        out_specs=[per_batch(r, c) for r, c, _ in outs] + [slot_spec] * 2 + [pl.BlockSpec((16, D), lambda b: (0, 0))],
        out_shape=[jax.ShapeDtypeStruct((batches, r, c), t) for r, c, t in outs]
        + [jax.ShapeDtypeStruct(slot_rows, F32)] * 2
        + [jax.ShapeDtypeStruct((16, D), F32)],
        scratch_shapes=[
            pltpu.VMEM((D, ff), BF16),
            pltpu.VMEM((ff, D), BF16),
            pltpu.VMEM((length, length), F32),
            pltpu.VMEM((length, D), F32),
            pltpu.VMEM((length, D), F32),
            pltpu.SemaphoreType.DMA((2,)),
        ],
        cost_estimate=LONG,
        compiler_params=pltpu.CompilerParams(vmem_limit_bytes=60 * MIB),
        name="forward_layer",
    )(tokens, segments, *small, w["inner"], w["outer"], *singles)


def attention_backward_kernel(q, k, v, do, stat, seg, *rest):
    dq_out, dk_out, dv_out, sums_out, mask = rest[-5:]
    length = q.shape[0]
    mask[...] = segment_mask(seg[...])
    low_half = lax.broadcasted_iota(jnp.int32, (length, 128), 1) < HEAD_DIM

    def head_pair(pair, carry):
        lanes = pl.ds(pl.multiple_of(pair * 128, 128), 128)
        q2 = q[:, lanes] * BF16(SCALE)
        k2 = k[:, lanes]
        v2 = v[:, lanes]
        do2 = do[:, lanes]
        k2t = (k2.astype(F32) * SCALE).T.astype(BF16)
        dqs, dks, dvs = [], [], []
        for h in range(2):
            half = low_half if h == 0 else ~low_half
            s = matmul_nt(jnp.where(half, k2, BF16(0)), q2) + mask[...]
            p = jnp.exp(s - stat[pl.ds(pair * 2 + h, 1), :])
            dp = matmul_nt(jnp.where(half, v2, BF16(0)), do2)
            pdp = p * dp
            delta = jnp.sum(pdp, axis=0, keepdims=True)
            ds = (pdp - p * delta).astype(BF16)
            dvs.append(matmul(p.astype(BF16), do2))
            dks.append(matmul(ds, q2))
            dqs.append(matmul(k2t[h * HEAD_DIM : (h + 1) * HEAD_DIM], ds))
        dq = jnp.concatenate(dqs, axis=0).T
        dk = jnp.where(low_half, dks[0], dks[1])
        dv = jnp.where(low_half, dvs[0], dvs[1])
        dq_out[:, lanes] = dq.astype(BF16)
        dk_out[:, lanes] = dk.astype(BF16)
        dv_out[:, lanes] = dv.astype(BF16)
        sums_out[0:1, lanes] = jnp.sum(dq, axis=0, keepdims=True)
        sums_out[1:2, lanes] = jnp.sum(dv, axis=0, keepdims=True)
        return carry

    lax.fori_loop(0, HEADS // 2, head_pair, 0)


def attention_backward(q, k, v, do, stat, segments, batch, into):
    batches, length, _ = q.shape

    def per_batch(rows, cols):
        return pl.BlockSpec((None, rows, cols), lambda i: (batch, 0, 0))

    wide = per_batch(length, D)
    shape = jax.ShapeDtypeStruct(q.shape, BF16)
    kept = pl.BlockSpec(memory_space=pl.ANY)
    return pl.pallas_call(
        attention_backward_kernel,
        grid=(1,),
        in_specs=[wide, wide, wide, wide, per_batch(16, length), per_batch(1, length)]
        + [kept] * len(into),
        out_specs=[wide, wide, wide, per_batch(8, D)],
        out_shape=[shape, shape, shape, jax.ShapeDtypeStruct((batches, 8, D), F32)],
        scratch_shapes=[pltpu.VMEM((length, length), F32)],
        input_output_aliases={6 + n: n for n in range(len(into))},
        cost_estimate=LONG,
        compiler_params=pltpu.CompilerParams(vmem_limit_bytes=48 * MIB),
        name="attention_backward",
    )(q, k, v, do, stat, segments, *into)


def first_backward_kernel(
    h2, d1, normed1, stat, vectors, w_inner, w_out, h1_out, d0_out, dm_out, sums_out
):
    length = h2.shape[0]
    upstream = h2[...] + matmul_nt(d1[...], w_inner[...])
    inv_std = jnp.broadcast_to(stat[HEADS : HEADS + 1, :], (128, length)).T[:, :1]
    normed = normed1[...].astype(F32)
    through = upstream * vectors[3:4]
    grad = inv_std * (
        through
        - jnp.mean(through, axis=-1, keepdims=True)
        - normed * jnp.mean(through * normed, axis=-1, keepdims=True)
    )
    h1_out[...] = grad
    low = grad.astype(BF16)
    d0_out[...] = low
    dm_out[...] = matmul_nt(low, w_out[...]).astype(BF16)

    @pl.when(pl.program_id(1) == 0)
    def _():
        sums_out[...] = jnp.zeros_like(sums_out)

    sums_out[0:1] += jnp.sum(grad, axis=0, keepdims=True)
    sums_out[1:2] += jnp.sum(upstream * normed, axis=0, keepdims=True)
    sums_out[2:3] += jnp.sum(upstream, axis=0, keepdims=True)


def first_backward(h2, d1, normed1, stat, vectors, w_inner, w_out):
    batches, length, _ = h2.shape
    ff = d1.shape[2]
    block = 512

    def rows(cols):
        return pl.BlockSpec((None, block, cols), lambda b, i: (b, i, 0))

    def whole(a):
        return pl.BlockSpec(a.shape, lambda b, i: (0, 0), pipeline_mode=pl.Buffered(1))

    return pl.pallas_call(
        first_backward_kernel,
        grid=(batches, length // block),
        in_specs=[
            rows(D), rows(ff), rows(D), pl.BlockSpec((None, 16, block), lambda b, i: (b, 0, i)),
            whole(vectors), whole(w_inner), whole(w_out),
        ],
        out_specs=[rows(D), rows(D), rows(D), pl.BlockSpec((None, 8, D), lambda b, i: (b, 0, 0))],
        out_shape=[
            jax.ShapeDtypeStruct(h2.shape, F32),
            jax.ShapeDtypeStruct(h2.shape, BF16),
            jax.ShapeDtypeStruct(h2.shape, BF16),
            jax.ShapeDtypeStruct((batches, 8, D), F32),
        ],
        cost_estimate=LONG,
        compiler_params=pltpu.CompilerParams(vmem_limit_bytes=48 * MIB),
        name="first_backward",
    )(h2, d1, normed1, stat, vectors, w_inner, w_out)


def pack_vectors(sums0, sums1, sums2, b_inner, rows):
    def kernel(attn, first, second, inner, out):
        out[...] = jnp.zeros_like(out)
        attn_sum = attn[0] + attn[1]
        first_sum = first[0] + first[1]
        second_sum = second[0] + second[1]
        out[0:2] = attn_sum[0:2]
        out[2:5] = first_sum[0:3]
        out[5:8] = second_sum[0:3]
        for n in range(inner.shape[1] // D):
            out[8 + n : 9 + n] = inner[:, n * D : (n + 1) * D]

    return pl.pallas_call(
        kernel, out_shape=jax.ShapeDtypeStruct((rows, D), F32), name="pack_vectors",
    )(sums0, sums1, sums2, b_inner)


def contrast_kernel(
    order, pairs_bits, counts, every, own, pooled, seg, loss_out, grad_out, pooled_grad_out
):
    rows = every.shape[0]
    everything = every[...]
    mine = own[...]
    me = lax.axis_index("pairs")
    my_stream = lax.axis_index("stream")
    my_core = me & 1

    def where_from(block):
        bit = {name: (block >> at) & 1 for at, name in enumerate(order)}
        core = my_core ^ bit["core"]
        straight = core == 0
        pair = me ^ bit["core"] ^ (jnp.where(straight, bit["xy"], bit["yx"]) << 1)
        for n in range(2, pairs_bits):
            pair = pair ^ (bit[n] << n)
        return my_stream ^ jnp.where(straight, bit["yx"], bit["xy"]), pair

    def batch_of(r):
        return (r >> 2) & 1

    r_col = lax.broadcasted_iota(jnp.int32, (rows, 1), 0)
    r_row = lax.broadcasted_iota(jnp.int32, (1, rows), 1)
    o_col = lax.broadcasted_iota(jnp.int32, (8, 1), 0)
    stream_col, pair_col = where_from(r_col >> 3)
    stream_row, pair_row = where_from(r_row >> 3)

    def count_step(p, carry):
        col, row = carry
        first, second = counts[0, p], counts[1, p]
        col = jnp.where(pair_col == p, jnp.where(batch_of(r_col) == 0, first, second), col)
        row = jnp.where(pair_row == p, jnp.where(batch_of(r_row) == 0, first, second), row)
        return col, row

    count_col, count_row = lax.fori_loop(
        0, 1 << pairs_bits, count_step, (jnp.zeros_like(r_col), jnp.zeros_like(r_row))
    )
    ok_col = (r_col & 3) < count_col
    ok_row = (r_row & 3) < count_row
    my_count = jnp.where(batch_of(o_col) == 0, counts[0, me], counts[1, me])
    my_ok = (o_col & 3) < my_count
    my_valid = my_ok.astype(F32)

    logits = dims(everything, everything, ((1,), (1,)), precision=HIGHEST) / LOGIT_DIVISOR
    related = (batch_of(r_col) == batch_of(r_row)) & (stream_col != stream_row) & ok_col
    masked = jnp.where(related, logits, NEG)
    top = jnp.max(masked, axis=0, keepdims=True)
    lse_row = top + jnp.log(jnp.sum(jnp.exp(masked - top), axis=0, keepdims=True))

    own_logits = dims(mine, everything, ((1,), (1,)), precision=HIGHEST) / LOGIT_DIVISOR
    other = (batch_of(o_col) == batch_of(r_row)) & (stream_row != my_stream)
    target = jnp.where(other & (pair_row == me) & ((o_col & 3) == (r_row & 3)), 1.0, 0.0)
    forward_logits = jnp.where(other & ok_row, own_logits, NEG)
    own_top = jnp.max(forward_logits, axis=1, keepdims=True)
    own_lse = own_top + jnp.log(
        jnp.sum(jnp.exp(forward_logits - own_top), axis=1, keepdims=True)
    )
    loss = (own_lse - jnp.sum(target * own_logits, axis=1, keepdims=True)) * my_valid
    loss_out[...] = jnp.broadcast_to(loss, loss_out.shape)
    forward_grad = (jnp.exp(forward_logits - own_lse) - target) * my_valid
    back_logits = jnp.where(other & my_ok, own_logits, NEG)
    back_grad = jnp.where(other & ok_row, jnp.exp(back_logits - lse_row) - target, 0.0)
    both = (forward_grad + back_grad) / LOGIT_DIVISOR
    grad = dims(both, everything, ((1,), (0,)), precision=HIGHEST)
    grad_out[...] = grad
    length = seg.shape[2]
    wide = (8, length)
    seg_rows = jnp.where(
        lax.broadcasted_iota(jnp.int32, wide, 0) < SLOTS,
        jnp.broadcast_to(seg[0], wide),
        jnp.broadcast_to(seg[1], wide),
    )
    in_slot = seg_rows == (lax.broadcasted_iota(jnp.int32, wide, 0) & 3)
    counted = jnp.sum(jnp.where(in_slot, 1.0, 0.0), axis=1, keepdims=True)
    pool = pooled[...]
    inv = lax.rsqrt(jnp.mean(pool * pool, axis=-1, keepdims=True) + UNIT_EPS)
    through = grad * D**-0.5
    inner = jnp.mean(pool * through, axis=-1, keepdims=True)
    pooled_grad_out[...] = (through * inv - pool * (inner * inv * inv * inv)) / counted


def contrast(order, pairs_bits, counts, every, own, pooled, seg):
    smem = pl.BlockSpec(memory_space=pltpu.SMEM)
    vmem = pl.BlockSpec(memory_space=pltpu.VMEM)
    return pl.pallas_call(
        functools.partial(contrast_kernel, order, pairs_bits),
        in_specs=[smem] + [vmem] * 4,
        out_specs=[vmem] * 3,
        out_shape=[
            jax.ShapeDtypeStruct((8, 128), F32),
            jax.ShapeDtypeStruct((8, D), F32),
            jax.ShapeDtypeStruct((8, D), F32),
        ],
        cost_estimate=LONG,
        compiler_params=pltpu.CompilerParams(vmem_limit_bytes=40 * MIB),
        name="contrast",
    )(counts, every, own, pooled, seg)


def norm2_backward_kernel(cot, normed2, stat, seg, pooled_grad, vectors, d2_out, grad_out, sums_out):
    length = cot.shape[0]
    batch = pl.program_id(0)
    columns = jnp.broadcast_to(stat[HEADS + 1 : HEADS + 2, :], (128, length)).T
    inv_std = columns[:, :1]
    seg_col = jnp.broadcast_to(seg[...].astype(F32), (128, length)).T[:, :1]
    spread = jnp.zeros((length, D), F32)
    for number in range(SLOTS):
        row = pooled_grad[pl.ds(batch * SLOTS + number, 1), :]
        spread = jnp.where(seg_col == float(number), row, spread)
    upstream = cot[...].astype(F32) + spread
    normed = normed2[...].astype(F32)
    through = upstream * vectors[6:7]
    grad = inv_std * (
        through
        - jnp.mean(through, axis=-1, keepdims=True)
        - normed * jnp.mean(through * normed, axis=-1, keepdims=True)
    )
    grad_out[...] = grad
    d2_out[...] = grad.astype(BF16)
    sums_out[0:1, :] = jnp.sum(grad, axis=0, keepdims=True)
    sums_out[1:2, :] = jnp.sum(upstream * normed, axis=0, keepdims=True)
    sums_out[2:3, :] = jnp.sum(upstream, axis=0, keepdims=True)


def norm2_backward(cot, normed2, stat, seg, pooled_grad, vectors):
    batches, length, _ = cot.shape

    def per_batch(rows, cols):
        return pl.BlockSpec((None, rows, cols), lambda b: (b, 0, 0))

    wide = per_batch(length, D)
    return pl.pallas_call(
        norm2_backward_kernel,
        grid=(batches,),
        in_specs=[
            wide, wide, per_batch(16, length), per_batch(1, length),
            pl.BlockSpec((8, D), lambda b: (0, 0)), pl.BlockSpec((16, D), lambda b: (0, 0)),
        ],
        out_specs=[wide, wide, per_batch(8, D)],
        out_shape=[
            jax.ShapeDtypeStruct(cot.shape, BF16),
            jax.ShapeDtypeStruct(cot.shape, F32),
            jax.ShapeDtypeStruct((batches, 8, D), F32),
        ],
        cost_estimate=LONG,
        compiler_params=pltpu.CompilerParams(vmem_limit_bytes=40 * MIB),
        name="norm2_backward",
    )(cot, normed2, stat, seg, pooled_grad, vectors)


def stages(pairs):
    bits = pairs.bit_length() - 1
    p = lax.axis_index("pairs")
    s = lax.axis_index("stream")
    core = p & 1

    def table(move):
        return [
            (a * pairs + b, move(a, b)[0] * pairs + move(a, b)[1])
            for a in range(2)
            for b in range(pairs)
        ]

    made = {
        "core": (core, table(lambda a, b: (a, b ^ 1))),
        "xy": (
            jnp.where(core == 0, (p >> 1) & 1, s),
            table(lambda a, b: (a, b ^ 2) if b % 2 == 0 else (a ^ 1, b)),
        ),
        "yx": (
            jnp.where(core == 0, s, (p >> 1) & 1),
            table(lambda a, b: (a ^ 1, b) if b % 2 == 0 else (a, b ^ 2)),
        ),
    }
    for n in range(2, bits):
        made[n] = ((p >> n) & 1, table(lambda a, b, n=n: (a, b ^ (1 << n))))
    return made


def send(value, permutation):
    return lax.ppermute(value, AXES, permutation)


def gather_all(value, steps, order):
    for at in range(0, len(order), 2):
        first = steps[order[at]][1]
        parts = [value, send(value, first)]
        if at + 1 < len(order):
            second = steps[order[at + 1]][1]
            onward = dict(second)
            parts.append(send(value, second))
            parts.append(send(value, [(source, onward[target]) for source, target in first]))
        value = jnp.concatenate(parts, axis=0)
    return value


def kernel_call(kernel, grid, in_specs, out_specs, out_shape, name, scratch=(), limit=48):
    return pl.pallas_call(
        kernel,
        grid_spec=pltpu.PrefetchScalarGridSpec(
            num_scalar_prefetch=1, grid=grid, in_specs=in_specs, out_specs=out_specs,
            scratch_shapes=scratch,
        ),
        out_shape=out_shape,
        cost_estimate=LONG,
        compiler_params=pltpu.CompilerParams(vmem_limit_bytes=limit * MIB),
        name=name,
    )


def block_rows(rows, columns):
    block = rows
    while block * columns * 4 > 3 * MIB and block % 16 == 0:
        block //= 2
    return block


def split_sum(x, y, bit):
    rows, columns = x.shape
    half = rows // 2
    block = block_rows(half, columns)
    n = half // block

    def kernel(b, xs, ys, xk, yk, give, keep):
        give[...] = xs[...] + ys[...]
        keep[...] = xk[...] + yk[...]

    other = pl.BlockSpec((block, columns), lambda i, b: ((1 - b[0]) * n + i, 0))
    own = pl.BlockSpec((block, columns), lambda i, b: (b[0] * n + i, 0))
    out = pl.BlockSpec((block, columns), lambda i, b: (i, 0))
    shape = jax.ShapeDtypeStruct((half, columns), F32)
    return kernel_call(
        kernel, (n,), [other, other, own, own], [out, out], [shape, shape], "split_sum"
    )(bit, x, y, x, y)


def join(own, got, bit):
    rows, columns = own.shape
    block = block_rows(rows, columns)
    n = rows // block

    def kernel(b, mine, other, out):
        @pl.when(pl.program_id(0) == 0)
        def _():
            out[...] = mine[...]

        @pl.when(pl.program_id(0) != 0)
        def _():
            out[...] = other[...]

    return kernel_call(
        kernel, (2, n),
        [
            pl.BlockSpec((block, columns), lambda j, i, b: (jnp.where(j == 0, i, n - 1), 0)),
            pl.BlockSpec((block, columns), lambda j, i, b: (jnp.where(j == 0, 0, i), 0)),
        ],
        pl.BlockSpec((block, columns), lambda j, i, b: (jnp.where(j == 0, b[0], 1 - b[0]) * n + i, 0)),
        jax.ShapeDtypeStruct((2 * rows, columns), F32), "join",
    )(bit, own, got)


def rearrange(inputs, bits, outputs, pieces, name):
    def kernel(at, *refs):
        sources, targets = refs[: len(inputs)], refs[len(inputs) :]

        def place(row, choice, rows):
            if choice is None:
                return pl.ds(row, rows)
            bit = at[choice[0]] if not choice[1] else 1 - at[choice[0]]
            return pl.ds(pl.multiple_of(row + bit * rows, 8), rows)

        for target, row, choice, rows, terms in pieces:
            total = None
            for source, start, pick in terms:
                value = sources[source][place(start, pick, rows), :]
                total = value if total is None else total + value
            targets[target][place(row, choice, rows), :] = total

    def whole(rows):
        return pl.BlockSpec((rows, D), lambda i, at: (0, 0))

    return kernel_call(
        kernel, (1,), [whole(a.shape[0]) for a in inputs], [whole(rows) for rows in outputs],
        [jax.ShapeDtypeStruct((rows, D), F32) for rows in outputs], name,
    )(jnp.stack(bits).astype(jnp.int32), *inputs)


def split_attention(total, blocks):
    deep = 2 * D // 3
    return total - deep, deep


def join_attention(own, got, bit, blocks):
    rows = own.shape[0]
    wide, deep = split_attention(rows, blocks)
    per = wide // blocks
    step = per - 8
    cut = blocks * step - D

    def kernel(b, own, got, query, key, value, out, vectors):
        def write(half, source, first, second):
            for n in range(blocks):
                piece = source[n * per : n * per + step]
                if n * step < D:
                    first[n * step : (n + 1) * step] = piece
                else:
                    second[n * step - D : (n + 1) * step - D] = piece
                vectors[half * blocks + n : half * blocks + n + 1] = source[
                    n * per + step : n * per + step + 1
                ]
            second[cut:] = source[wide:]

        @pl.when(b[0] == 0)
        def _():
            write(0, own, query, key)
            write(1, got, value, out)

        @pl.when(b[0] != 0)
        def _():
            write(0, got, query, key)
            write(1, own, value, out)

    def whole(count):
        return pl.BlockSpec((count, D), lambda i, b: (0, 0))

    return kernel_call(
        kernel, (1,), [whole(rows)] * 2, [whole(D)] * 4 + [whole(2 * blocks)],
        [jax.ShapeDtypeStruct((D, D), F32)] * 4 + [jax.ShapeDtypeStruct((2 * blocks, D), F32)],
        "join_attention",
    )(bit, own, got)


def outer_grad_half(act, d2, half):
    tokens, ff = act.shape
    n = ff // 2 // D

    def kernel(b, left, right, out):
        out[...] = matmul_tn(left[...], right[...])

    return kernel_call(
        kernel, (n,),
        [pl.BlockSpec((tokens, D), lambda i, b: (0, b[0] * n + i)), pl.BlockSpec((tokens, D), lambda i, b: (0, 0))],
        pl.BlockSpec((D, D), lambda i, b: (i, 0)),
        jax.ShapeDtypeStruct((ff // 2, D), F32), "outer_grad",
    )(half, act, d2)


def inner_grad_half(first, d1, half):
    tokens, ff = d1.shape
    n = ff // 2 // D

    def kernel(b, left, right, out):
        out[...] = matmul_tn(left[...], right[...])

    return kernel_call(
        kernel, (n,),
        [pl.BlockSpec((tokens, D), lambda i, b: (0, 0)), pl.BlockSpec((tokens, D), lambda i, b: (0, b[0] * n + i))],
        pl.BlockSpec((D, D), lambda i, b: (i, 0)),
        jax.ShapeDtypeStruct((ff // 2, D), F32), "inner_grad",
    )(half, first, d1)


def grad_split(wide, left, right, got, which):
    tokens = left.shape[0]

    def kernel(b, left, right, got, give, keep):
        total = matmul_tn(left[...], right[...]) + got[...]

        @pl.when(pl.program_id(0) == 0)
        def _():
            give[...] = total

        @pl.when(pl.program_id(0) != 0)
        def _():
            keep[...] = total

    def pick(i, b):
        return jnp.where(i == 0, 1 - b[1], b[1])

    moving = pl.BlockSpec((tokens, D), lambda i, b: (0, b[0] * 2 + pick(i, b)))
    still = pl.BlockSpec((tokens, D), lambda i, b: (0, 0))
    block = pl.BlockSpec((D, D), lambda i, b: (0, 0))
    shape = jax.ShapeDtypeStruct((D, D), F32)
    return kernel_call(
        kernel, (2,),
        [moving if wide else still, still if wide else moving, pl.BlockSpec((D, D), lambda i, b: (pick(i, b), 0))],
        [block, block], [shape, shape], "grad_split",
    )(which, left, right, got)


def join_into(own, got, bits, across):
    rows, columns = own.shape
    block = block_rows(rows, columns)
    n = rows // block

    def kernel(b, mine, other, out, final):
        @pl.when(pl.program_id(0) == 0)
        def _():
            out[...] = mine[...]
            final[...] = mine[...]

        @pl.when(pl.program_id(0) != 0)
        def _():
            out[...] = other[...]
            final[...] = other[...]

    def at(j, i, b):
        return jnp.where(j == 0, b[0], 1 - b[0]) * n + i

    per = D // block

    def final_at(j, i, b):
        row = b[1] * 2 * n + at(j, i, b)
        return (row % per, row // per) if across else (row, 0)

    shape = (D, 4 * rows // D * D) if across else (4 * rows, columns)
    return kernel_call(
        kernel, (2, n),
        [
            pl.BlockSpec((block, columns), lambda j, i, b: (jnp.where(j == 0, i, n - 1), 0)),
            pl.BlockSpec((block, columns), lambda j, i, b: (jnp.where(j == 0, 0, i), 0)),
        ],
        [
            pl.BlockSpec((block, columns), lambda j, i, b: (at(j, i, b), 0)),
            pl.BlockSpec((block, columns), final_at),
        ],
        [jax.ShapeDtypeStruct((2 * rows, columns), F32), jax.ShapeDtypeStruct(shape, F32)], "join_into",
    )(bits, own, got)


def place(got, final, bit, across):
    rows, columns = got.shape
    block = block_rows(D, columns)
    n = rows // block
    per = D // block

    def kernel(b, other, _, out):
        out[...] = other[...]

    def at(i, b):
        row = (1 - b[0]) * n + i
        return (row % per, row // per) if across else (row, 0)

    return pl.pallas_call(
        kernel,
        grid_spec=pltpu.PrefetchScalarGridSpec(
            num_scalar_prefetch=1, grid=(n,),
            in_specs=[
                pl.BlockSpec((block, columns), lambda i, b: (i, 0)), pl.BlockSpec(memory_space=pl.ANY)
            ],
            out_specs=pl.BlockSpec((block, columns), at),
        ),
        out_shape=jax.ShapeDtypeStruct(final.shape, F32),
        input_output_aliases={2: 0},
        cost_estimate=LONG,
        compiler_params=pltpu.CompilerParams(vmem_limit_bytes=48 * MIB),
        name="place",
    )(bit, got, final)


def attention_grad_half(x, mixed, dq, dk, dv, d0, vectors, half):
    tokens = x.shape[0]
    blocks = vectors.shape[0] // 2
    cut = 4 * D // 3 - D
    step = (D + cut) // blocks
    per = step + 8

    wide = blocks * per

    def kernel(b, x, mixed, dq, dk, dv, d0, vectors, out):
        def write(first, second, base):
            for n in range(blocks):
                start = n * step
                piece = first[start : start + step] if start < D else second[start - D : start - D + step]
                out[n * per : n * per + step] = piece
                out[n * per + step : (n + 1) * per] = jnp.broadcast_to(
                    vectors[base + n : base + n + 1], (8, D)
                )
            out[wide:] = second[cut:]

        @pl.when(b[0] == 0)
        def _():
            write(matmul_tn(x[...], dq[...]), matmul_tn(x[...], dk[...]), 0)

        @pl.when(b[0] != 0)
        def _():
            write(matmul_tn(x[...], dv[...]), matmul_tn(mixed[...], d0[...]), blocks)

    def whole(rows):
        return pl.BlockSpec((rows, D), lambda i, b: (0, 0))

    return kernel_call(
        kernel, (1,), [whole(tokens)] * 6 + [whole(2 * blocks)], whole(wide + D - cut),
        jax.ShapeDtypeStruct((wide + D - cut, D), F32),
        "attention_grad",
    )(half, x, mixed, dq, dk, dv, d0, vectors)


class Line:
    def __init__(self, **start):
        self.at = dict(start)
        self.last = []

    def step(self, function, given, made):
        names = list(dict.fromkeys(list(given) + self.last))
        held = lax.optimization_barrier([self.at[name] for name in names])
        self.at.update(zip(names, held))
        got = function(*[self.at[name] for name in given])
        self.at.update(zip(made, got))
        self.last = list(made)


class Sum:
    def __init__(self, line, name, steps, route, last, across, result):
        self.line, self.name, self.steps = line, name, steps
        self.route, self.swap, self.across, self.result = route, last, across, result
        self.visits = 0

    def bit(self, step):
        return self.steps[step][0].reshape(1).astype(jnp.int32)

    def start(self, give):
        self.line.at[self.name + ".got"] = send(give, self.steps[self.route[0]][1])

    def visit(self):
        line, route = self.line, self.route
        keep, got = self.name + ".keep", self.name + ".got"
        n, at = len(route), self.visits
        self.visits += 1
        if at < n - 1:
            bit = self.bit(route[at + 1])
            line.step(lambda k, g: split_sum(k, g, bit), [keep, got], [self.name + ".give", keep])
            self.line.at[got] = send(self.line.at[self.name + ".give"], self.steps[route[at + 1]][1])
        elif at <= n:
            line.step(lambda k, g: (k + g,), [keep, got], [keep])
            step = self.swap if at == n - 1 else route[n - 1]
            self.line.at[got] = send(self.line.at[keep], self.steps[step][1])
        elif at < 2 * n:
            step = route[2 * n - at]
            bit = self.bit(step)
            if at == 2 * n - 1:
                bits = jnp.concatenate([bit, self.bit(route[0])])
                line.step(
                    lambda k, g: join_into(k, g, bits, self.across), [keep, got], [keep, self.name + ".all"]
                )
            else:
                line.step(lambda k, g: (join(k, g, bit),), [keep, got], [keep])
            self.line.at[got] = send(self.line.at[keep], self.steps[route[2 * n - at - 1]][1])
        else:
            bit = self.bit(route[0])
            line.step(
                lambda g, final: (place(g, final, bit, self.across),), [got, self.name + ".all"], [self.result]
            )

    def keep_and_split(self, wide, given):
        self.visits = 1
        which = jnp.concatenate([self.bit(self.route[0]), self.bit(self.route[1])])
        made = [self.name + ".give", self.name + ".keep"]
        self.line.step(
            lambda a, b, got: grad_split(wide, a, b, got, which), given + [self.name + ".got"], made
        )
        self.line.at[self.name + ".got"] = send(self.line.at[made[0]], self.steps[self.route[1]][1])


class PairSum:
    def __init__(self, line, name, steps, routes, last, finish, results):
        self.line, self.name, self.steps = line, name, steps
        self.routes, self.swap, self.finish, self.results = routes, last, finish, results
        self.visits = 0
        self.names = []

    def start(self, give, rows):
        self.rows = list(rows)
        self.line.at[self.name + ".got0"] = send(give, self.steps["core"][1])
        self.got = [(self.name + ".got0", 0), (self.name + ".got0", rows[0])]
        self.keep = [(self.name + ".keep", 0), (self.name + ".keep", rows[0])]

    def plan(self, step_names, rows):
        if step_names[0] == step_names[1]:
            return [(0, 0), (0, rows[0])], [rows[0] + rows[1]], [step_names[0]]
        return [(0, 0), (1, 0)], list(rows), list(step_names)

    def go(self, pieces_of, out_rows, sends, made):
        names = []
        for part in self.keep + self.got:
            if part[0] not in names:
                names.append(part[0])
        pieces, bits = pieces_of(names)
        if not bits:
            bits = [self.steps["core"][0]]
        self.line.step(
            lambda *a: rearrange(a, bits, out_rows, pieces, "rearrange"), names, made
        )
        for name, step, got in sends:
            self.line.at[got] = send(self.line.at[name], self.steps[step][1])

    def visit(self):
        line, n, at = self.line, len(self.routes[0]), self.visits
        tag = f"{self.name}.{at}."
        self.visits += 1
        if at == 2 * n:
            bit = self.steps["core"][0].reshape(1).astype(jnp.int32)
            line.step(
                lambda k, g: self.finish(k, g, bit), [self.keep[0][0], self.got[0][0]], self.results
            )
            return
        if at < n - 1:
            after = [route[at + 1] for route in self.routes]
            half = [rows // 2 for rows in self.rows]
            where, outs, steps = self.plan(after, half)
            made = [tag + f"give{i}" for i in range(len(outs))] + [tag + "keep0", tag + "keep1"]

            def pieces_of(names):
                pieces, bits = [], []
                for part in range(2):
                    bits.append(self.steps[after[part]][0])
                    for flip, (target, row) in ((True, where[part]), (False, (len(outs) + part, 0))):
                        terms = [
                            (names.index(source[part][0]), source[part][1], (part, flip))
                            for source in (self.keep, self.got)
                        ]
                        pieces.append((target, row, None, half[part], terms))
                return pieces, bits

            sends = [(made[i], steps[i], tag + f"got{i}") for i in range(len(outs))]
            self.go(pieces_of, outs + half, sends, made)
            self.rows = half
            self.keep = [(tag + "keep0", 0), (tag + "keep1", 0)]
            self.got = [(tag + f"got{where[part][0]}", where[part][1]) for part in range(2)]
            return
        if at <= n:
            after = [self.swap] * 2 if at == n - 1 else [route[n - 1] for route in self.routes]
            rows, grown = self.rows, self.rows
        else:
            back = [route[2 * n - at] for route in self.routes]
            after = [route[2 * n - at - 1] for route in self.routes]
            rows, grown = self.rows, [2 * r for r in self.rows]
        where, outs, steps = self.plan(after, grown)
        made = [tag + f"own{i}" for i in range(len(outs))]

        def pieces_of(names):
            pieces, bits = [], []
            for part in range(2):
                target, row = where[part]
                mine, other = (
                    (names.index(source[part][0]), source[part][1], None) for source in (self.keep, self.got)
                )
                if at <= n:
                    pieces.append((target, row, None, rows[part], [mine, other]))
                else:
                    bits.append(self.steps[back[part]][0])
                    pieces.append((target, row, (part, False), rows[part], [mine]))
                    pieces.append((target, row, (part, True), rows[part], [other]))
            return pieces, bits

        sends = [(made[i], steps[i], tag + f"got{i}") for i in range(len(outs))]
        self.go(pieces_of, outs, sends, made)
        self.rows = list(grown)
        self.keep = [(tag + f"own{where[part][0]}", where[part][1]) for part in range(2)]
        self.got = [(tag + f"got{where[part][0]}", where[part][1]) for part in range(2)]


def on_device(
    tokens, segments, counts, cotangent, w_query, b_query, w_key, w_value, b_value, w_out, b_out,
    gain_attn, bias_attn, w_inner, b_inner, w_outer, b_outer, gain_ffn, bias_ffn,
):
    pairs = lax.axis_size("pairs")
    bits = pairs.bit_length() - 1
    batches, length = tokens.shape[1], tokens.shape[2]
    ff = w_inner.shape[1]
    stream = lax.axis_index("stream")
    pair = lax.axis_index("pairs")
    steps = stages(pairs)
    w = dict(
        query=w_query, b_query=b_query, key=w_key, value=w_value, b_value=b_value, out=w_out,
        b_out=b_out, gain1=gain_attn, shift1=bias_attn, inner=w_inner, b_inner=b_inner,
        outer=w_outer, b_outer=b_outer, gain2=gain_ffn, shift2=bias_ffn,
    )
    x = tokens[0]
    seg = segments[0]
    order = list(range(bits - 1, 1, -1)) + ["xy", "yx", "core"]
    singles = [b_query, b_value, b_out, gain_attn, bias_attn, b_outer, gain_ffn, bias_ffn, b_inner]
    (
        q, k, v, mixed, stat, first_low, normed1, act, slope, normed2, hidden, pooled, unit, vectors
    ) = forward(x, seg, singles, w)
    every = gather_all(unit, steps, order)
    loss, unit_grad, pooled_grad = contrast(
        order, bits, counts, every, unit, pooled, seg
    )
    loss = loss[:, 0].reshape(1, batches, SLOTS)
    d2, grad_h2, sums2 = norm2_backward(cotangent[0], normed2, stat, seg, pooled_grad, vectors)

    tokens_all = batches * length
    flat = lambda a: a.reshape(tokens_all, a.shape[-1])
    core = steps["core"][0].reshape(1).astype(jnp.int32)
    line = Line(
        d2=flat(d2), act=flat(act), slope=flat(slope), h2=grad_h2, first=flat(first_low),
        normed1=normed1, q=q,
    )
    middle = list(range(3, bits - 1))
    flat_route = ["core", "xy", "yx", 2] + middle
    deep_route = ["core", 2, "yx", "xy"] + middle
    last = bits - 1
    blocks = 1 << len(flat_route)
    outer = Sum(line, "outer", steps, flat_route, last, False, "total_outer")
    inner = Sum(line, "inner", steps, flat_route, last, True, "total_inner")
    rest = PairSum(
        line, "rest", steps, (flat_route, deep_route), last,
        lambda k, g, b: join_attention(k, g, b, blocks // 2),
        ["total_query", "total_key", "total_value", "total_out", "vectors"],
    )
    xf, mixed_f = flat(x), flat(mixed)

    def give(group, function, given):
        name = group.name + ".give"
        line.step(lambda *a: (function(*a, 1 - core),), given, [name])
        if group is rest:
            group.start(line.at[name], split_attention(line.at[name].shape[0], blocks // 2))
        else:
            group.start(line.at[name])

    def keep(group, function, given):
        line.step(lambda *a: (function(*a, core),), given, [group.name + ".keep"])

    def inner_step(d2, slope):
        grad_inner = matmul_nt(d2, w_outer) * slope.astype(F32)
        return grad_inner.astype(BF16), jnp.sum(grad_inner, axis=0, keepdims=True)

    def first_step(d1, h2, normed):
        d1 = d1.reshape(batches, length, ff)
        h1, d0, dm, sums = first_backward(h2, d1, normed, stat, vectors, w_inner, w_out)
        return flat(h1), flat(d0), dm, sums

    def attention(batch):
        names = ["dq", "dk", "dv", "sums0"]
        into = names if batch else []
        line.step(
            lambda q, dm, *into: attention_backward(q, k, v, dm, stat, seg, batch, into),
            ["q", "dm"] + into, names,
        )

    def attention_grads(d0, dq, dk, dv, vectors, half):
        return attention_grad_half(xf, mixed_f, flat(dq), flat(dk), flat(dv), d0, vectors, half)

    attention_given = ["d0", "dq", "dk", "dv", "vec"]

    def token_gradient(h1, dq, dk, dv):
        return (
            (
                h1
                + matmul_nt(flat(dq), w_query)
                + matmul_nt(flat(dk), w_key)
                + matmul_nt(flat(dv), w_value)
            ).astype(BF16),
        )

    def vector_step():
        line.step(
            lambda a, b, c: (pack_vectors(a, b, sums2, c, blocks),), ["sums0", "sums1", "b_inner"], ["vec"]
        )

    actions = {
        "gw1s": lambda: give(outer, outer_grad_half, ["act", "d2"]),
        "gw1k": lambda: outer.keep_and_split(True, ["act", "d2"]),
        "B2": lambda: line.step(inner_step, ["d2", "slope"], ["d1", "b_inner"]),
        "gw2s": lambda: give(inner, inner_grad_half, ["first", "d1"]),
        "gw2k": lambda: inner.keep_and_split(False, ["first", "d1"]),
        "B3": lambda: line.step(first_step, ["d1", "h2", "normed1"], ["h1", "d0", "dm", "sums1"]),
        "at0": lambda: attention(0),
        "at1": lambda: attention(1),
        "gw3s": lambda: give(rest, attention_grads, attention_given),
        "gw3k": lambda: keep(rest, attention_grads, attention_given),
        "tok": lambda: line.step(token_gradient, ["h1", "dq", "dk", "dv"], ["tokens"]),
        "v": vector_step,
        "0": outer.visit,
        "1": inner.visit,
        "2": rest.visit,
    }
    for action in ORDER:
        actions[action]()
    for group in (inner, outer, rest):
        while group.visits < 2 * len(flat_route) + 1:
            group.visit()
    total = line.at
    sums = total["vectors"]
    return (
        loss,
        unit.reshape(1, batches, SLOTS, D),
        unit_grad.reshape(1, batches, SLOTS, D),
        hidden[None],
        total["tokens"].reshape(1, batches, length, D),
        total["total_query"],
        sums[0],
        total["total_key"],
        total["total_value"],
        sums[1],
        total["total_out"],
        sums[2],
        sums[3],
        sums[4],
        total["total_inner"],
        sums[8 : 8 + ff // D].reshape(ff),
        total["total_outer"],
        sums[5],
        sums[6],
        sums[7],
    )


def solution(mesh):
    row = P("stream", None, "pairs", None)
    in_specs = (row, row, P(), row) + (P(),) * 15
    out_specs = (P("stream", None, "pairs"), row, row, row, row) + (P(),) * 15
    return jax.shard_map(
        on_device, mesh=mesh, in_specs=in_specs, out_specs=out_specs, check_vma=False
    )
```

```python
import functools
import jax
import jax.numpy as jnp
import numpy as np
from jax import lax
from jax.experimental import pallas as pl
from jax.experimental.pallas import tpu as pltpu
from jax.sharding import PartitionSpec as P

D = 768
HEADS = 12
HEAD_DIM = 64
SLOTS = 4
AXES = ("stream", "pairs")
F32 = jnp.float32
BF16 = jnp.bfloat16
HIGHEST = lax.Precision.HIGHEST
LOGIT_DIVISOR = 0.01
NORM_EPS = 1e-12
UNIT_EPS = 1e-06
NEG = -1000000000.0
SCALE = HEAD_DIM**-0.5
FF_CHUNK = 1536
MIB = 1 << 20
LONG = pl.CostEstimate(flops=1 << 44, bytes_accessed=1 << 38, transcendentals=0)

ORDER = (
    "gw1s", "B2", "gw1k", "B3", "at0", "gw2s", "0", "gw2k",
    "0", "at1", "0", "v", "1", "gw3s", "1", "gw3k",
    "0", "2", "0", "1", "2", "0", "1", "2",
    "1", "2", "1", "0", "2", "tok", "2", "0",
    "1", "2", "2", "1", "2",
)

TAIL_P = 0.305
TAIL = (
    0.12163973223592059,
    0.12246682364852957,
    0.10342082369335875,
    0.12102182071723708,
    -0.03797709812500149,
    0.18571719569775694,
    -0.15298848174013205,
    0.0366992308655468,
)


def dims(lhs, rhs, contract, **kw):
    return lax.dot_general(lhs, rhs, (contract, ((), ())), preferred_element_type=F32, **kw)


def matmul(lhs, rhs):
    return dims(lhs, rhs, ((1,), (0,)))


def matmul_nt(lhs, rhs):
    return dims(lhs, rhs, ((1,), (1,)))


def matmul_tn(lhs, rhs):
    return dims(lhs, rhs, ((0,), (0,)))


def norm_forward(total):
    centered = total - jnp.mean(total, axis=-1, keepdims=True)
    inv_std = lax.rsqrt(jnp.mean(centered * centered, axis=-1, keepdims=True) + NORM_EPS)
    return centered * inv_std, inv_std


def gelu_both(x):
    tail = 1.0 / (1.0 + TAIL_P * jnp.abs(x))
    poly = jnp.full_like(x, TAIL[-1])
    for coefficient in TAIL[-2::-1]:
        poly = poly * tail + coefficient
    bell = jnp.exp(-0.5 * (x * x))
    lower = poly * tail * bell
    phi = jnp.where(x >= 0, 1.0 - lower, lower)
    return x * phi, phi + x * bell * 0.3989422804014327


def segment_mask(seg_row):
    length = seg_row.shape[1]
    rows = jnp.broadcast_to(seg_row.astype(F32), (128, length))
    columns = rows.T
    wide = jnp.concatenate([columns] * (length // 128), axis=1)
    return jnp.where(wide == jnp.broadcast_to(seg_row.astype(F32), (length, length)), 0.0, NEG)


def forward_kernel(*refs):
    tokens, seg, wq, wk, wv, wo, wi_hbm, wo2_hbm = refs[:8]
    singles = refs[8:17]
    (
        q_out, k_out, v_out, mixed_out, stat_out, first_out, normed1_out, act_out, slope_out,
        normed2_out, hidden_out, pooled_out, unit_out, vectors, wi, wo2, mask, first_f32, acc, act_held,
        slope_held, sem, out_sem,
    ) = refs[17:]
    copy_in = pltpu.make_async_copy(wi_hbm, wi, sem.at[0])
    copy_out = pltpu.make_async_copy(wo2_hbm, wo2, sem.at[1])

    @pl.when(pl.program_id(0) == 0)
    def _():
        copy_in.start()
        copy_out.start()
        for row, single in enumerate(singles):
            for n in range(single.shape[0] // D):
                vectors[row + n : row + n + 1] = (
                    single[n * D : (n + 1) * D].astype(F32).reshape(1, D)
                )

    x = tokens[...]
    length = x.shape[0]
    q_out[...] = (matmul(x, wq[...]) + vectors[0:1]).astype(BF16)
    k_out[...] = matmul(x, wk[...]).astype(BF16)
    v_out[...] = (matmul(x, wv[...]) + vectors[1:2]).astype(BF16)
    mask[...] = segment_mask(seg[...])
    low_half = lax.broadcasted_iota(jnp.int32, (length, 128), 1) < HEAD_DIM

    def head_pair(pair, carry):
        lanes = pl.ds(pl.multiple_of(pair * 128, 128), 128)
        q2 = q_out[:, lanes] * BF16(SCALE)
        k2 = k_out[:, lanes]
        v2 = v_out[:, lanes].astype(F32).T.astype(BF16)
        outs = []
        for h in range(2):
            kh = jnp.where(low_half if h == 0 else ~low_half, k2, BF16(0))
            s = matmul_nt(kh, q2) + mask[...]
            top = jnp.max(s, axis=0, keepdims=True)
            e = jnp.exp(s - top)
            total = jnp.sum(e, axis=0, keepdims=True)
            o = matmul(v2[h * HEAD_DIM : (h + 1) * HEAD_DIM], e.astype(BF16)) * (1.0 / total)
            outs.append(o)
            stat_out[pl.ds(pair * 2 + h, 1), :] = top + jnp.log(total)
        mixed_out[:, lanes] = jnp.concatenate(outs, axis=0).T.astype(BF16)
        return carry

    lax.fori_loop(0, HEADS // 2, head_pair, 0, unroll=3)
    total = x.astype(F32) + (matmul(mixed_out[...], wo[...]) + vectors[2:3])
    normed1, inv1 = norm_forward(total)
    normed1_out[...] = normed1.astype(normed1_out.dtype)
    first = normed1 * vectors[3:4] + vectors[4:5]
    first_f32[...] = first
    first_out[...] = first.astype(BF16)

    @pl.when(pl.program_id(0) == 0)
    def _():
        copy_in.wait()
        copy_out.wait()

    acc[...] = jnp.zeros_like(acc)
    leaving = []
    for chunk in range(wi.shape[1] // FF_CHUNK):
        lanes = pl.ds(chunk * FF_CHUNK, FF_CHUNK)
        row = 8 + chunk * (FF_CHUNK // D)
        shift = jnp.concatenate([vectors[row + n : row + n + 1] for n in range(FF_CHUNK // D)], axis=1)
        inner = matmul(first_out[...], wi[:, lanes]) + shift
        act, slope = gelu_both(inner)
        act = act.astype(BF16)
        act_held[:, lanes] = act
        slope_held[:, lanes] = slope.astype(BF16)
        for held, out in ((act_held, act_out), (slope_held, slope_out)):
            leaving.append(
                pltpu.make_async_copy(
                    held.at[:, lanes], out.at[pl.program_id(0), :, lanes], out_sem.at[len(leaving)]
                )
            )
            leaving[-1].start()
        acc[...] += matmul(act, wo2[lanes, :])

    normed2, inv2 = norm_forward(first_f32[...] + (acc[...] + vectors[5:6]))
    normed2_out[...] = normed2.astype(normed2_out.dtype)
    hidden = normed2 * vectors[6:7] + vectors[7:8]
    hidden_out[...] = hidden.astype(BF16)
    slots = lax.broadcasted_iota(jnp.int32, (8, length), 0)
    one_hot = jnp.where(jnp.broadcast_to(seg[...], (8, length)) == slots, 1.0, 0.0)
    counted = jnp.maximum(jnp.sum(one_hot, axis=1, keepdims=True), 1.0)
    pooled = dims(one_hot, hidden, ((1,), (0,)), precision=HIGHEST) / counted
    pooled = pooled[:SLOTS]
    unit = (
        pooled * lax.rsqrt(jnp.mean(pooled * pooled, axis=-1, keepdims=True) + UNIT_EPS) * D**-0.5
    )
    for batch in range(pooled_out.shape[0] // SLOTS):

        @pl.when(pl.program_id(0) == batch)
        def _(batch=batch):
            pooled_out[batch * SLOTS : (batch + 1) * SLOTS] = pooled
            unit_out[batch * SLOTS : (batch + 1) * SLOTS] = unit

    stat_out[pl.ds(HEADS, 1), :] = jnp.broadcast_to(inv1, (length, 128)).T[:1]
    stat_out[pl.ds(HEADS + 1, 1), :] = jnp.broadcast_to(inv2, (length, 128)).T[:1]
    for copy in leaving:
        copy.wait()


def forward(tokens, segments, singles, w):
    batches, length, _ = tokens.shape
    ff = w["inner"].shape[1]

    def per_batch(rows, cols):
        return pl.BlockSpec((None, rows, cols), lambda b: (b, 0, 0))

    def whole(a):
        return pl.BlockSpec(a.shape, lambda b: (0,) * a.ndim, pipeline_mode=pl.Buffered(1))

    hbm = pl.BlockSpec(memory_space=pl.ANY)
    small = [w["query"], w["key"], w["value"], w["out"]]
    outs = [
        (length, D, BF16), (length, D, BF16), (length, D, BF16), (length, D, BF16),
        (16, length, F32), (length, D, BF16), (length, D, BF16), (length, ff, BF16),
        (length, ff, BF16), (length, D, BF16), (length, D, BF16),
    ]
    slot_rows = (batches * SLOTS, D)
    slot_spec = pl.BlockSpec(slot_rows, lambda b: (0, 0))
    return pl.pallas_call(
        forward_kernel,
        grid=(batches,),
        in_specs=[per_batch(length, D), per_batch(1, length)]
        + [whole(a) for a in small]
        + [hbm, hbm]
        + [whole(a) for a in singles],
        out_specs=[hbm if c == ff else per_batch(r, c) for r, c, _ in outs]
        + [slot_spec] * 2 + [pl.BlockSpec((16, D), lambda b: (0, 0))],
        out_shape=[jax.ShapeDtypeStruct((batches, r, c), t) for r, c, t in outs]
        + [jax.ShapeDtypeStruct(slot_rows, F32)] * 2
        + [jax.ShapeDtypeStruct((16, D), F32)],
        scratch_shapes=[
            pltpu.VMEM((D, ff), BF16),
            pltpu.VMEM((ff, D), BF16),
            pltpu.VMEM((length, length), F32),
            pltpu.VMEM((length, D), F32),
            pltpu.VMEM((length, D), F32),
            pltpu.VMEM((length, ff), BF16),
            pltpu.VMEM((length, ff), BF16),
            pltpu.SemaphoreType.DMA((2,)),
            pltpu.SemaphoreType.DMA((2 * ff // FF_CHUNK,)),
        ],
        cost_estimate=LONG,
        compiler_params=pltpu.CompilerParams(vmem_limit_bytes=60 * MIB),
        name="forward_layer",
    )(tokens, segments, *small, w["inner"], w["outer"], *singles)


def attention_backward_kernel(q, k, v, do, stat, seg, *rest):
    dq_out, dk_out, dv_out, sums_out, mask = rest[-5:]
    length = q.shape[0]
    mask[...] = segment_mask(seg[...])
    low_half = lax.broadcasted_iota(jnp.int32, (length, 128), 1) < HEAD_DIM

    def head_pair(pair, carry):
        lanes = pl.ds(pl.multiple_of(pair * 128, 128), 128)
        q2 = q[:, lanes] * BF16(SCALE)
        k2 = k[:, lanes]
        v2 = v[:, lanes]
        do2 = do[:, lanes]
        k2t = (k2.astype(F32) * SCALE).T.astype(BF16)
        dqs, dks, dvs = [], [], []
        for h in range(2):
            half = low_half if h == 0 else ~low_half
            s = matmul_nt(jnp.where(half, k2, BF16(0)), q2) + mask[...]
            p = jnp.exp(s - stat[pl.ds(pair * 2 + h, 1), :])
            dp = matmul_nt(jnp.where(half, v2, BF16(0)), do2)
            pdp = p * dp
            delta = jnp.sum(pdp, axis=0, keepdims=True)
            ds = (pdp - p * delta).astype(BF16)
            dvs.append(matmul(p.astype(BF16), do2))
            dks.append(matmul(ds, q2))
            dqs.append(matmul(k2t[h * HEAD_DIM : (h + 1) * HEAD_DIM], ds))
        dq = jnp.concatenate(dqs, axis=0).T
        dk = jnp.where(low_half, dks[0], dks[1])
        dv = jnp.where(low_half, dvs[0], dvs[1])
        dq_out[:, lanes] = dq.astype(BF16)
        dk_out[:, lanes] = dk.astype(BF16)
        dv_out[:, lanes] = dv.astype(BF16)
        sums_out[0:1, lanes] = jnp.sum(dq, axis=0, keepdims=True)
        sums_out[1:2, lanes] = jnp.sum(dv, axis=0, keepdims=True)
        return carry

    lax.fori_loop(0, HEADS // 2, head_pair, 0)


def attention_backward(q, k, v, do, stat, segments, batch, into):
    batches, length, _ = q.shape

    def per_batch(rows, cols):
        return pl.BlockSpec((None, rows, cols), lambda i: (batch, 0, 0))

    wide = per_batch(length, D)
    shape = jax.ShapeDtypeStruct(q.shape, BF16)
    kept = pl.BlockSpec(memory_space=pl.ANY)
    return pl.pallas_call(
        attention_backward_kernel,
        grid=(1,),
        in_specs=[wide, wide, wide, wide, per_batch(16, length), per_batch(1, length)]
        + [kept] * len(into),
        out_specs=[wide, wide, wide, per_batch(8, D)],
        out_shape=[shape, shape, shape, jax.ShapeDtypeStruct((batches, 8, D), F32)],
        scratch_shapes=[pltpu.VMEM((length, length), F32)],
        input_output_aliases={6 + n: n for n in range(len(into))},
        cost_estimate=LONG,
        compiler_params=pltpu.CompilerParams(vmem_limit_bytes=48 * MIB),
        name="attention_backward",
    )(q, k, v, do, stat, segments, *into)


def first_backward_kernel(
    h2, d1, normed1, stat, vectors, w_inner, w_out, h1_out, d0_out, dm_out, sums_out
):
    length = h2.shape[0]
    upstream = h2[...] + matmul_nt(d1[...], w_inner[...])
    inv_std = jnp.broadcast_to(stat[HEADS : HEADS + 1, :], (128, length)).T[:, :1]
    normed = normed1[...].astype(F32)
    through = upstream * vectors[3:4]
    grad = inv_std * (
        through
        - jnp.mean(through, axis=-1, keepdims=True)
        - normed * jnp.mean(through * normed, axis=-1, keepdims=True)
    )
    h1_out[...] = grad
    low = grad.astype(BF16)
    d0_out[...] = low
    dm_out[...] = matmul_nt(low, w_out[...]).astype(BF16)

    @pl.when(pl.program_id(1) == 0)
    def _():
        sums_out[...] = jnp.zeros_like(sums_out)

    sums_out[0:1] += jnp.sum(grad, axis=0, keepdims=True)
    sums_out[1:2] += jnp.sum(upstream * normed, axis=0, keepdims=True)
    sums_out[2:3] += jnp.sum(upstream, axis=0, keepdims=True)


def first_backward(h2, d1, normed1, stat, vectors, w_inner, w_out):
    batches, length, _ = h2.shape
    ff = d1.shape[2]
    block = 512

    def rows(cols):
        return pl.BlockSpec((None, block, cols), lambda b, i: (b, i, 0))

    def whole(a):
        return pl.BlockSpec(a.shape, lambda b, i: (0, 0), pipeline_mode=pl.Buffered(1))

    return pl.pallas_call(
        first_backward_kernel,
        grid=(batches, length // block),
        in_specs=[
            rows(D), rows(ff), rows(D), pl.BlockSpec((None, 16, block), lambda b, i: (b, 0, i)),
            whole(vectors), whole(w_inner), whole(w_out),
        ],
        out_specs=[rows(D), rows(D), rows(D), pl.BlockSpec((None, 8, D), lambda b, i: (b, 0, 0))],
        out_shape=[
            jax.ShapeDtypeStruct(h2.shape, F32),
            jax.ShapeDtypeStruct(h2.shape, BF16),
            jax.ShapeDtypeStruct(h2.shape, BF16),
            jax.ShapeDtypeStruct((batches, 8, D), F32),
        ],
        cost_estimate=LONG,
        compiler_params=pltpu.CompilerParams(vmem_limit_bytes=48 * MIB),
        name="first_backward",
    )(h2, d1, normed1, stat, vectors, w_inner, w_out)


def pack_vectors(sums0, sums1, sums2, b_inner, rows):
    def kernel(attn, first, second, inner, out):
        out[...] = jnp.zeros_like(out)
        attn_sum = attn[0] + attn[1]
        first_sum = first[0] + first[1]
        second_sum = second[0] + second[1]
        out[0:2] = attn_sum[0:2]
        out[2:5] = first_sum[0:3]
        out[5:8] = second_sum[0:3]
        for n in range(inner.shape[1] // D):
            out[8 + n : 9 + n] = inner[:, n * D : (n + 1) * D]

    return pl.pallas_call(
        kernel, out_shape=jax.ShapeDtypeStruct((rows, D), F32), name="pack_vectors",
    )(sums0, sums1, sums2, b_inner)


def contrast_kernel(
    order, pairs_bits, counts, every, own, pooled, seg, loss_out, grad_out, pooled_grad_out
):
    rows = every.shape[0]
    everything = every[...]
    mine = own[...]
    me = lax.axis_index("pairs")
    my_stream = lax.axis_index("stream")
    my_core = me & 1

    def where_from(block):
        bit = {name: (block >> at) & 1 for at, name in enumerate(order)}
        core = my_core ^ bit["core"]
        straight = core == 0
        pair = me ^ bit["core"] ^ (jnp.where(straight, bit["xy"], bit["yx"]) << 1)
        for n in range(2, pairs_bits):
            pair = pair ^ (bit[n] << n)
        return my_stream ^ jnp.where(straight, bit["yx"], bit["xy"]), pair

    def batch_of(r):
        return (r >> 2) & 1

    r_col = lax.broadcasted_iota(jnp.int32, (rows, 1), 0)
    r_row = lax.broadcasted_iota(jnp.int32, (1, rows), 1)
    o_col = lax.broadcasted_iota(jnp.int32, (8, 1), 0)
    stream_col, pair_col = where_from(r_col >> 3)
    stream_row, pair_row = where_from(r_row >> 3)

    def count_step(p, carry):
        col, row = carry
        first, second = counts[0, p], counts[1, p]
        col = jnp.where(pair_col == p, jnp.where(batch_of(r_col) == 0, first, second), col)
        row = jnp.where(pair_row == p, jnp.where(batch_of(r_row) == 0, first, second), row)
        return col, row

    count_col, count_row = lax.fori_loop(
        0, 1 << pairs_bits, count_step, (jnp.zeros_like(r_col), jnp.zeros_like(r_row))
    )
    ok_col = (r_col & 3) < count_col
    ok_row = (r_row & 3) < count_row
    my_count = jnp.where(batch_of(o_col) == 0, counts[0, me], counts[1, me])
    my_ok = (o_col & 3) < my_count
    my_valid = my_ok.astype(F32)

    logits = dims(everything, everything, ((1,), (1,)), precision=HIGHEST) / LOGIT_DIVISOR
    related = (batch_of(r_col) == batch_of(r_row)) & (stream_col != stream_row) & ok_col
    masked = jnp.where(related, logits, NEG)
    top = jnp.max(masked, axis=0, keepdims=True)
    lse_row = top + jnp.log(jnp.sum(jnp.exp(masked - top), axis=0, keepdims=True))

    own_logits = dims(mine, everything, ((1,), (1,)), precision=HIGHEST) / LOGIT_DIVISOR
    other = (batch_of(o_col) == batch_of(r_row)) & (stream_row != my_stream)
    target = jnp.where(other & (pair_row == me) & ((o_col & 3) == (r_row & 3)), 1.0, 0.0)
    forward_logits = jnp.where(other & ok_row, own_logits, NEG)
    own_top = jnp.max(forward_logits, axis=1, keepdims=True)
    own_lse = own_top + jnp.log(
        jnp.sum(jnp.exp(forward_logits - own_top), axis=1, keepdims=True)
    )
    loss = (own_lse - jnp.sum(target * own_logits, axis=1, keepdims=True)) * my_valid
    loss_out[...] = jnp.broadcast_to(loss, loss_out.shape)
    forward_grad = (jnp.exp(forward_logits - own_lse) - target) * my_valid
    back_logits = jnp.where(other & my_ok, own_logits, NEG)
    back_grad = jnp.where(other & ok_row, jnp.exp(back_logits - lse_row) - target, 0.0)
    both = (forward_grad + back_grad) / LOGIT_DIVISOR
    grad = dims(both, everything, ((1,), (0,)), precision=HIGHEST)
    grad_out[...] = grad
    length = seg.shape[2]
    wide = (8, length)
    seg_rows = jnp.where(
        lax.broadcasted_iota(jnp.int32, wide, 0) < SLOTS,
        jnp.broadcast_to(seg[0], wide),
        jnp.broadcast_to(seg[1], wide),
    )
    in_slot = seg_rows == (lax.broadcasted_iota(jnp.int32, wide, 0) & 3)
    counted = jnp.sum(jnp.where(in_slot, 1.0, 0.0), axis=1, keepdims=True)
    pool = pooled[...]
    inv = lax.rsqrt(jnp.mean(pool * pool, axis=-1, keepdims=True) + UNIT_EPS)
    through = grad * D**-0.5
    inner = jnp.mean(pool * through, axis=-1, keepdims=True)
    pooled_grad_out[...] = (through * inv - pool * (inner * inv * inv * inv)) / counted


def contrast(order, pairs_bits, counts, every, own, pooled, seg):
    smem = pl.BlockSpec(memory_space=pltpu.SMEM)
    vmem = pl.BlockSpec(memory_space=pltpu.VMEM)
    return pl.pallas_call(
        functools.partial(contrast_kernel, order, pairs_bits),
        in_specs=[smem] + [vmem] * 4,
        out_specs=[vmem] * 3,
        out_shape=[
            jax.ShapeDtypeStruct((8, 128), F32),
            jax.ShapeDtypeStruct((8, D), F32),
            jax.ShapeDtypeStruct((8, D), F32),
        ],
        cost_estimate=LONG,
        compiler_params=pltpu.CompilerParams(vmem_limit_bytes=40 * MIB),
        name="contrast",
    )(counts, every, own, pooled, seg)


def norm2_backward_kernel(cot, normed2, stat, seg, pooled_grad, vectors, d2_out, grad_out, sums_out):
    length = cot.shape[0]
    batch = pl.program_id(0)
    columns = jnp.broadcast_to(stat[HEADS + 1 : HEADS + 2, :], (128, length)).T
    inv_std = columns[:, :1]
    seg_col = jnp.broadcast_to(seg[...].astype(F32), (128, length)).T[:, :1]
    spread = jnp.zeros((length, D), F32)
    for number in range(SLOTS):
        row = pooled_grad[pl.ds(batch * SLOTS + number, 1), :]
        spread = jnp.where(seg_col == float(number), row, spread)
    upstream = cot[...].astype(F32) + spread
    normed = normed2[...].astype(F32)
    through = upstream * vectors[6:7]
    grad = inv_std * (
        through
        - jnp.mean(through, axis=-1, keepdims=True)
        - normed * jnp.mean(through * normed, axis=-1, keepdims=True)
    )
    grad_out[...] = grad
    d2_out[...] = grad.astype(BF16)
    sums_out[0:1, :] = jnp.sum(grad, axis=0, keepdims=True)
    sums_out[1:2, :] = jnp.sum(upstream * normed, axis=0, keepdims=True)
    sums_out[2:3, :] = jnp.sum(upstream, axis=0, keepdims=True)


def norm2_backward(cot, normed2, stat, seg, pooled_grad, vectors):
    batches, length, _ = cot.shape

    def per_batch(rows, cols):
        return pl.BlockSpec((None, rows, cols), lambda b: (b, 0, 0))

    wide = per_batch(length, D)
    return pl.pallas_call(
        norm2_backward_kernel,
        grid=(batches,),
        in_specs=[
            wide, wide, per_batch(16, length), per_batch(1, length),
            pl.BlockSpec((8, D), lambda b: (0, 0)), pl.BlockSpec((16, D), lambda b: (0, 0)),
        ],
        out_specs=[wide, wide, per_batch(8, D)],
        out_shape=[
            jax.ShapeDtypeStruct(cot.shape, BF16),
            jax.ShapeDtypeStruct(cot.shape, F32),
            jax.ShapeDtypeStruct((batches, 8, D), F32),
        ],
        cost_estimate=LONG,
        compiler_params=pltpu.CompilerParams(vmem_limit_bytes=40 * MIB),
        name="norm2_backward",
    )(cot, normed2, stat, seg, pooled_grad, vectors)


def stages(pairs):
    bits = pairs.bit_length() - 1
    p = lax.axis_index("pairs")
    s = lax.axis_index("stream")
    core = p & 1

    def table(move):
        return [
            (a * pairs + b, move(a, b)[0] * pairs + move(a, b)[1])
            for a in range(2)
            for b in range(pairs)
        ]

    made = {
        "core": (core, table(lambda a, b: (a, b ^ 1))),
        "xy": (
            jnp.where(core == 0, (p >> 1) & 1, s),
            table(lambda a, b: (a, b ^ 2) if b % 2 == 0 else (a ^ 1, b)),
        ),
        "yx": (
            jnp.where(core == 0, s, (p >> 1) & 1),
            table(lambda a, b: (a ^ 1, b) if b % 2 == 0 else (a, b ^ 2)),
        ),
    }
    for n in range(2, bits):
        made[n] = ((p >> n) & 1, table(lambda a, b, n=n: (a, b ^ (1 << n))))
    return made


def send(value, permutation):
    return lax.ppermute(value, AXES, permutation)


def gather_all(value, steps, order):
    for at in range(0, len(order), 2):
        first = steps[order[at]][1]
        parts = [value, send(value, first)]
        if at + 1 < len(order):
            second = steps[order[at + 1]][1]
            onward = dict(second)
            parts.append(send(value, second))
            parts.append(send(value, [(source, onward[target]) for source, target in first]))
        value = jnp.concatenate(parts, axis=0)
    return value


def kernel_call(kernel, grid, in_specs, out_specs, out_shape, name, scratch=(), limit=48):
    return pl.pallas_call(
        kernel,
        grid_spec=pltpu.PrefetchScalarGridSpec(
            num_scalar_prefetch=1, grid=grid, in_specs=in_specs, out_specs=out_specs,
            scratch_shapes=scratch,
        ),
        out_shape=out_shape,
        cost_estimate=LONG,
        compiler_params=pltpu.CompilerParams(vmem_limit_bytes=limit * MIB),
        name=name,
    )


def block_rows(rows, columns):
    block = rows
    while block * columns * 4 > 3 * MIB and block % 16 == 0:
        block //= 2
    return block


def split_sum(x, y, bit):
    rows, columns = x.shape
    half = rows // 2
    block = block_rows(half, columns)
    n = half // block

    def kernel(b, xs, ys, xk, yk, give, keep):
        give[...] = xs[...] + ys[...]
        keep[...] = xk[...] + yk[...]

    other = pl.BlockSpec((block, columns), lambda i, b: ((1 - b[0]) * n + i, 0))
    own = pl.BlockSpec((block, columns), lambda i, b: (b[0] * n + i, 0))
    out = pl.BlockSpec((block, columns), lambda i, b: (i, 0))
    shape = jax.ShapeDtypeStruct((half, columns), F32)
    return kernel_call(
        kernel, (n,), [other, other, own, own], [out, out], [shape, shape], "split_sum"
    )(bit, x, y, x, y)


def join(own, got, bit):
    rows, columns = own.shape
    block = block_rows(rows, columns)
    n = rows // block

    def kernel(b, mine, other, out):
        @pl.when(pl.program_id(0) == 0)
        def _():
            out[...] = mine[...]

        @pl.when(pl.program_id(0) != 0)
        def _():
            out[...] = other[...]

    return kernel_call(
        kernel, (2, n),
        [
            pl.BlockSpec((block, columns), lambda j, i, b: (jnp.where(j == 0, i, n - 1), 0)),
            pl.BlockSpec((block, columns), lambda j, i, b: (jnp.where(j == 0, 0, i), 0)),
        ],
        pl.BlockSpec((block, columns), lambda j, i, b: (jnp.where(j == 0, b[0], 1 - b[0]) * n + i, 0)),
        jax.ShapeDtypeStruct((2 * rows, columns), F32), "join",
    )(bit, own, got)


def rearrange(inputs, bits, outputs, pieces, name):
    def kernel(at, *refs):
        sources, targets = refs[: len(inputs)], refs[len(inputs) :]

        def place(row, choice, rows):
            if choice is None:
                return pl.ds(row, rows)
            bit = at[choice[0]] if not choice[1] else 1 - at[choice[0]]
            return pl.ds(pl.multiple_of(row + bit * rows, 8), rows)

        for target, row, choice, rows, terms in pieces:
            total = None
            for source, start, pick in terms:
                value = sources[source][place(start, pick, rows), :]
                total = value if total is None else total + value
            targets[target][place(row, choice, rows), :] = total

    def whole(rows):
        return pl.BlockSpec((rows, D), lambda i, at: (0, 0))

    return kernel_call(
        kernel, (1,), [whole(a.shape[0]) for a in inputs], [whole(rows) for rows in outputs],
        [jax.ShapeDtypeStruct((rows, D), F32) for rows in outputs], name,
    )(jnp.stack(bits).astype(jnp.int32), *inputs)


def split_attention(total, blocks):
    deep = 2 * D // 3
    return total - deep, deep


def join_attention(own, got, bit, blocks):
    rows = own.shape[0]
    wide, deep = split_attention(rows, blocks)
    per = wide // blocks
    step = per - 8
    cut = blocks * step - D

    def kernel(b, own, got, query, key, value, out, vectors):
        def write(half, source, first, second):
            for n in range(blocks):
                piece = source[n * per : n * per + step]
                if n * step < D:
                    first[n * step : (n + 1) * step] = piece
                else:
                    second[n * step - D : (n + 1) * step - D] = piece
                vectors[half * blocks + n : half * blocks + n + 1] = source[
                    n * per + step : n * per + step + 1
                ]
            second[cut:] = source[wide:]

        @pl.when(b[0] == 0)
        def _():
            write(0, own, query, key)
            write(1, got, value, out)

        @pl.when(b[0] != 0)
        def _():
            write(0, got, query, key)
            write(1, own, value, out)

    def whole(count):
        return pl.BlockSpec((count, D), lambda i, b: (0, 0))

    return kernel_call(
        kernel, (1,), [whole(rows)] * 2, [whole(D)] * 4 + [whole(2 * blocks)],
        [jax.ShapeDtypeStruct((D, D), F32)] * 4 + [jax.ShapeDtypeStruct((2 * blocks, D), F32)],
        "join_attention",
    )(bit, own, got)


def outer_grad_half(act, d2, half):
    tokens, ff = act.shape
    n = ff // 2 // D

    def kernel(b, left, right, out):
        out[...] = matmul_tn(left[...], right[...])

    return kernel_call(
        kernel, (n,),
        [pl.BlockSpec((tokens, D), lambda i, b: (0, b[0] * n + i)), pl.BlockSpec((tokens, D), lambda i, b: (0, 0))],
        pl.BlockSpec((D, D), lambda i, b: (i, 0)),
        jax.ShapeDtypeStruct((ff // 2, D), F32), "outer_grad",
    )(half, act, d2)


def inner_grad_half(first, d1, half):
    tokens, ff = d1.shape
    n = ff // 2 // D

    def kernel(b, left, right, out):
        out[...] = matmul_tn(left[...], right[...])

    return kernel_call(
        kernel, (n,),
        [pl.BlockSpec((tokens, D), lambda i, b: (0, 0)), pl.BlockSpec((tokens, D), lambda i, b: (0, b[0] * n + i))],
        pl.BlockSpec((D, D), lambda i, b: (i, 0)),
        jax.ShapeDtypeStruct((ff // 2, D), F32), "inner_grad",
    )(half, first, d1)


def grad_split(wide, left, right, got, which):
    tokens = left.shape[0]

    def kernel(b, left, right, got, give, keep):
        total = matmul_tn(left[...], right[...]) + got[...]

        @pl.when(pl.program_id(0) == 0)
        def _():
            give[...] = total

        @pl.when(pl.program_id(0) != 0)
        def _():
            keep[...] = total

    def pick(i, b):
        return jnp.where(i == 0, 1 - b[1], b[1])

    moving = pl.BlockSpec((tokens, D), lambda i, b: (0, b[0] * 2 + pick(i, b)))
    still = pl.BlockSpec((tokens, D), lambda i, b: (0, 0))
    block = pl.BlockSpec((D, D), lambda i, b: (0, 0))
    shape = jax.ShapeDtypeStruct((D, D), F32)
    return kernel_call(
        kernel, (2,),
        [moving if wide else still, still if wide else moving, pl.BlockSpec((D, D), lambda i, b: (pick(i, b), 0))],
        [block, block], [shape, shape], "grad_split",
    )(which, left, right, got)


def join_into(own, got, bits, across):
    rows, columns = own.shape
    block = block_rows(rows, columns)
    n = rows // block

    def kernel(b, mine, other, out, final):
        @pl.when(pl.program_id(0) == 0)
        def _():
            out[...] = mine[...]
            final[...] = mine[...]

        @pl.when(pl.program_id(0) != 0)
        def _():
            out[...] = other[...]
            final[...] = other[...]

    def at(j, i, b):
        return jnp.where(j == 0, b[0], 1 - b[0]) * n + i

    per = D // block

    def final_at(j, i, b):
        row = b[1] * 2 * n + at(j, i, b)
        return (row % per, row // per) if across else (row, 0)

    shape = (D, 4 * rows // D * D) if across else (4 * rows, columns)
    return kernel_call(
        kernel, (2, n),
        [
            pl.BlockSpec((block, columns), lambda j, i, b: (jnp.where(j == 0, i, n - 1), 0)),
            pl.BlockSpec((block, columns), lambda j, i, b: (jnp.where(j == 0, 0, i), 0)),
        ],
        [
            pl.BlockSpec((block, columns), lambda j, i, b: (at(j, i, b), 0)),
            pl.BlockSpec((block, columns), final_at),
        ],
        [jax.ShapeDtypeStruct((2 * rows, columns), F32), jax.ShapeDtypeStruct(shape, F32)], "join_into",
    )(bits, own, got)


def place(got, final, bit, across):
    rows, columns = got.shape
    block = block_rows(D, columns)
    n = rows // block
    per = D // block

    def kernel(b, other, _, out):
        out[...] = other[...]

    def at(i, b):
        row = (1 - b[0]) * n + i
        return (row % per, row // per) if across else (row, 0)

    return pl.pallas_call(
        kernel,
        grid_spec=pltpu.PrefetchScalarGridSpec(
            num_scalar_prefetch=1, grid=(n,),
            in_specs=[
                pl.BlockSpec((block, columns), lambda i, b: (i, 0)), pl.BlockSpec(memory_space=pl.ANY)
            ],
            out_specs=pl.BlockSpec((block, columns), at),
        ),
        out_shape=jax.ShapeDtypeStruct(final.shape, F32),
        input_output_aliases={2: 0},
        cost_estimate=LONG,
        compiler_params=pltpu.CompilerParams(vmem_limit_bytes=48 * MIB),
        name="place",
    )(bit, got, final)


def attention_grad_half(x, mixed, dq, dk, dv, d0, vectors, half):
    tokens = x.shape[0]
    blocks = vectors.shape[0] // 2
    cut = 4 * D // 3 - D
    step = (D + cut) // blocks
    per = step + 8

    wide = blocks * per

    def kernel(b, x, mixed, dq, dk, dv, d0, vectors, out, left0, right0, left1, right1, sem):
        def copies(sources):
            return [
                pltpu.make_async_copy(source, held, sem.at[n])
                for n, (source, held) in enumerate(zip(sources, (left0, right0, left1, right1)))
            ]

        @pl.when(b[0] == 0)
        def _():
            for copy in copies((x, dq, x, dk)):
                copy.start()

        @pl.when(b[0] != 0)
        def _():
            for copy in copies((x, dv, mixed, d0)):
                copy.start()

        waits = copies((x, dq, x, dk))
        base = b[0] * blocks
        waits[0].wait()
        waits[1].wait()
        first = matmul_tn(left0[...], right0[...])
        waits[2].wait()
        waits[3].wait()
        second = matmul_tn(left1[...], right1[...])
        for n in range(blocks):
            start = n * step
            piece = first[start : start + step] if start < D else second[start - D : start - D + step]
            out[n * per : n * per + step] = piece
            out[n * per + step : (n + 1) * per] = jnp.broadcast_to(
                vectors[pl.ds(base + n, 1)], (8, D)
            )
        out[wide:] = second[cut:]

    def whole(rows):
        return pl.BlockSpec((rows, D), lambda i, b: (0, 0))

    hbm = pl.BlockSpec(memory_space=pl.ANY)
    return kernel_call(
        kernel, (1,), [hbm] * 6 + [whole(2 * blocks)], whole(wide + D - cut),
        jax.ShapeDtypeStruct((wide + D - cut, D), F32), "attention_grad",
        [pltpu.VMEM((tokens, D), BF16)] * 4 + [pltpu.SemaphoreType.DMA((4,))],
    )(half, x, mixed, dq, dk, dv, d0, vectors)


def grad_split(wide, left, right, got, which):
    tokens = left.shape[0]

    def kernel(b, left, right, got, give, keep):
        total = matmul_tn(left[...], right[...]) + got[...]

        @pl.when(pl.program_id(0) == 0)
        def _():
            give[...] = total

        @pl.when(pl.program_id(0) != 0)
        def _():
            keep[...] = total

    def pick(i, b):
        return jnp.where(i == 0, 1 - b[1], b[1])

    moving = pl.BlockSpec((tokens, D), lambda i, b: (0, b[0] * 2 + pick(i, b)))
    still = pl.BlockSpec((tokens, D), lambda i, b: (0, 0))
    block = pl.BlockSpec((D, D), lambda i, b: (0, 0))
    shape = jax.ShapeDtypeStruct((D, D), F32)
    return kernel_call(
        kernel, (2,),
        [moving if wide else still, still if wide else moving, pl.BlockSpec((D, D), lambda i, b: (pick(i, b), 0))],
        [block, block], [shape, shape], "grad_split",
    )(which, left, right, got)


def join_into(own, got, bits, across):
    rows, columns = own.shape
    block = block_rows(rows, columns)
    n = rows // block

    def kernel(b, mine, other, out, final):
        @pl.when(pl.program_id(0) == 0)
        def _():
            out[...] = mine[...]
            final[...] = mine[...]

        @pl.when(pl.program_id(0) != 0)
        def _():
            out[...] = other[...]
            final[...] = other[...]

    def at(j, i, b):
        return jnp.where(j == 0, b[0], 1 - b[0]) * n + i

    per = D // block

    def final_at(j, i, b):
        row = b[1] * 2 * n + at(j, i, b)
        return (row % per, row // per) if across else (row, 0)

    shape = (D, 4 * rows // D * D) if across else (4 * rows, columns)
    return kernel_call(
        kernel, (2, n),
        [
            pl.BlockSpec((block, columns), lambda j, i, b: (jnp.where(j == 0, i, n - 1), 0)),
            pl.BlockSpec((block, columns), lambda j, i, b: (jnp.where(j == 0, 0, i), 0)),
        ],
        [
            pl.BlockSpec((block, columns), lambda j, i, b: (at(j, i, b), 0)),
            pl.BlockSpec((block, columns), final_at),
        ],
        [jax.ShapeDtypeStruct((2 * rows, columns), F32), jax.ShapeDtypeStruct(shape, F32)], "join_into",
    )(bits, own, got)


def place(got, final, bit, across):
    rows, columns = got.shape
    block = block_rows(D, columns)
    n = rows // block
    per = D // block

    def kernel(b, other, _, out):
        out[...] = other[...]

    def at(i, b):
        row = (1 - b[0]) * n + i
        return (row % per, row // per) if across else (row, 0)

    return pl.pallas_call(
        kernel,
        grid_spec=pltpu.PrefetchScalarGridSpec(
            num_scalar_prefetch=1, grid=(n,),
            in_specs=[
                pl.BlockSpec((block, columns), lambda i, b: (i, 0)), pl.BlockSpec(memory_space=pl.ANY)
            ],
            out_specs=pl.BlockSpec((block, columns), at),
        ),
        out_shape=jax.ShapeDtypeStruct(final.shape, F32),
        input_output_aliases={2: 0},
        cost_estimate=LONG,
        compiler_params=pltpu.CompilerParams(vmem_limit_bytes=48 * MIB),
        name="place",
    )(bit, got, final)


def attention_grad_half(x, mixed, dq, dk, dv, d0, vectors, half):
    tokens = x.shape[0]
    blocks = vectors.shape[0] // 2
    cut = 4 * D // 3 - D
    step = (D + cut) // blocks
    per = step + 8

    wide = blocks * per

    def kernel(b, x, mixed, dq, dk, dv, d0, vectors, out):
        def write(first, second, base):
            for n in range(blocks):
                start = n * step
                piece = first[start : start + step] if start < D else second[start - D : start - D + step]
                out[n * per : n * per + step] = piece
                out[n * per + step : (n + 1) * per] = jnp.broadcast_to(
                    vectors[base + n : base + n + 1], (8, D)
                )
            out[wide:] = second[cut:]

        @pl.when(b[0] == 0)
        def _():
            write(matmul_tn(x[...], dq[...]), matmul_tn(x[...], dk[...]), 0)

        @pl.when(b[0] != 0)
        def _():
            write(matmul_tn(x[...], dv[...]), matmul_tn(mixed[...], d0[...]), blocks)

    def whole(rows):
        return pl.BlockSpec((rows, D), lambda i, b: (0, 0))

    return kernel_call(
        kernel, (1,), [whole(tokens)] * 6 + [whole(2 * blocks)], whole(wide + D - cut),
        jax.ShapeDtypeStruct((wide + D - cut, D), F32),
        "attention_grad",
    )(half, x, mixed, dq, dk, dv, d0, vectors)


class Line:
    def __init__(self, **start):
        self.at = dict(start)
        self.last = []

    def step(self, function, given, made):
        names = list(dict.fromkeys(list(given) + self.last))
        held = lax.optimization_barrier([self.at[name] for name in names])
        self.at.update(zip(names, held))
        got = function(*[self.at[name] for name in given])
        self.at.update(zip(made, got))
        self.last = list(made)


class Sum:
    def __init__(self, line, name, steps, route, last, across, result):
        self.line, self.name, self.steps = line, name, steps
        self.route, self.swap, self.across, self.result = route, last, across, result
        self.visits = 0

    def bit(self, step):
        return self.steps[step][0].reshape(1).astype(jnp.int32)

    def start(self, give):
        self.line.at[self.name + ".got"] = send(give, self.steps[self.route[0]][1])

    def visit(self):
        line, route = self.line, self.route
        keep, got = self.name + ".keep", self.name + ".got"
        n, at = len(route), self.visits
        self.visits += 1
        if at < n - 1:
            bit = self.bit(route[at + 1])
            line.step(lambda k, g: split_sum(k, g, bit), [keep, got], [self.name + ".give", keep])
            self.line.at[got] = send(self.line.at[self.name + ".give"], self.steps[route[at + 1]][1])
        elif at <= n:
            line.step(lambda k, g: (k + g,), [keep, got], [keep])
            step = self.swap if at == n - 1 else route[n - 1]
            self.line.at[got] = send(self.line.at[keep], self.steps[step][1])
        elif at < 2 * n:
            step = route[2 * n - at]
            bit = self.bit(step)
            if at == 2 * n - 1:
                bits = jnp.concatenate([bit, self.bit(route[0])])
                line.step(
                    lambda k, g: join_into(k, g, bits, self.across), [keep, got], [keep, self.name + ".all"]
                )
            else:
                line.step(lambda k, g: (join(k, g, bit),), [keep, got], [keep])
            self.line.at[got] = send(self.line.at[keep], self.steps[route[2 * n - at - 1]][1])
        else:
            bit = self.bit(route[0])
            line.step(
                lambda g, final: (place(g, final, bit, self.across),), [got, self.name + ".all"], [self.result]
            )

    def keep_and_split(self, wide, given):
        self.visits = 1
        which = jnp.concatenate([self.bit(self.route[0]), self.bit(self.route[1])])
        made = [self.name + ".give", self.name + ".keep"]
        self.line.step(
            lambda a, b, got: grad_split(wide, a, b, got, which), given + [self.name + ".got"], made
        )
        self.line.at[self.name + ".got"] = send(self.line.at[made[0]], self.steps[self.route[1]][1])


class PairSum:
    def __init__(self, line, name, steps, routes, last, finish, results):
        self.line, self.name, self.steps = line, name, steps
        self.routes, self.swap, self.finish, self.results = routes, last, finish, results
        self.visits = 0
        self.names = []

    def start(self, give, rows):
        self.rows = list(rows)
        self.line.at[self.name + ".got0"] = send(give, self.steps["core"][1])
        self.got = [(self.name + ".got0", 0), (self.name + ".got0", rows[0])]
        self.keep = [(self.name + ".keep", 0), (self.name + ".keep", rows[0])]

    def plan(self, step_names, rows):
        if step_names[0] == step_names[1]:
            return [(0, 0), (0, rows[0])], [rows[0] + rows[1]], [step_names[0]]
        return [(0, 0), (1, 0)], list(rows), list(step_names)

    def go(self, pieces_of, out_rows, sends, made):
        names = []
        for part in self.keep + self.got:
            if part[0] not in names:
                names.append(part[0])
        pieces, bits = pieces_of(names)
        if not bits:
            bits = [self.steps["core"][0]]
        self.line.step(
            lambda *a: rearrange(a, bits, out_rows, pieces, "rearrange"), names, made
        )
        for name, step, got in sends:
            self.line.at[got] = send(self.line.at[name], self.steps[step][1])

    def visit(self):
        line, n, at = self.line, len(self.routes[0]), self.visits
        tag = f"{self.name}.{at}."
        self.visits += 1
        if at == 2 * n:
            bit = self.steps["core"][0].reshape(1).astype(jnp.int32)
            line.step(
                lambda k, g: self.finish(k, g, bit), [self.keep[0][0], self.got[0][0]], self.results
            )
            return
        if at < n - 1:
            after = [route[at + 1] for route in self.routes]
            half = [rows // 2 for rows in self.rows]
            where, outs, steps = self.plan(after, half)
            made = [tag + f"give{i}" for i in range(len(outs))] + [tag + "keep0", tag + "keep1"]

            def pieces_of(names):
                pieces, bits = [], []
                for part in range(2):
                    bits.append(self.steps[after[part]][0])
                    for flip, (target, row) in ((True, where[part]), (False, (len(outs) + part, 0))):
                        terms = [
                            (names.index(source[part][0]), source[part][1], (part, flip))
                            for source in (self.keep, self.got)
                        ]
                        pieces.append((target, row, None, half[part], terms))
                return pieces, bits

            sends = [(made[i], steps[i], tag + f"got{i}") for i in range(len(outs))]
            self.go(pieces_of, outs + half, sends, made)
            self.rows = half
            self.keep = [(tag + "keep0", 0), (tag + "keep1", 0)]
            self.got = [(tag + f"got{where[part][0]}", where[part][1]) for part in range(2)]
            return
        if at <= n:
            after = [self.swap] * 2 if at == n - 1 else [route[n - 1] for route in self.routes]
            rows, grown = self.rows, self.rows
        else:
            back = [route[2 * n - at] for route in self.routes]
            after = [route[2 * n - at - 1] for route in self.routes]
            rows, grown = self.rows, [2 * r for r in self.rows]
        where, outs, steps = self.plan(after, grown)
        made = [tag + f"own{i}" for i in range(len(outs))]

        def pieces_of(names):
            pieces, bits = [], []
            for part in range(2):
                target, row = where[part]
                mine, other = (
                    (names.index(source[part][0]), source[part][1], None) for source in (self.keep, self.got)
                )
                if at <= n:
                    pieces.append((target, row, None, rows[part], [mine, other]))
                else:
                    bits.append(self.steps[back[part]][0])
                    pieces.append((target, row, (part, False), rows[part], [mine]))
                    pieces.append((target, row, (part, True), rows[part], [other]))
            return pieces, bits

        sends = [(made[i], steps[i], tag + f"got{i}") for i in range(len(outs))]
        self.go(pieces_of, outs, sends, made)
        self.rows = list(grown)
        self.keep = [(tag + f"own{where[part][0]}", where[part][1]) for part in range(2)]
        self.got = [(tag + f"got{where[part][0]}", where[part][1]) for part in range(2)]


def on_device(
    tokens, segments, counts, cotangent, w_query, b_query, w_key, w_value, b_value, w_out, b_out,
    gain_attn, bias_attn, w_inner, b_inner, w_outer, b_outer, gain_ffn, bias_ffn,
):
    pairs = lax.axis_size("pairs")
    bits = pairs.bit_length() - 1
    batches, length = tokens.shape[1], tokens.shape[2]
    ff = w_inner.shape[1]
    stream = lax.axis_index("stream")
    pair = lax.axis_index("pairs")
    steps = stages(pairs)
    w = dict(
        query=w_query, b_query=b_query, key=w_key, value=w_value, b_value=b_value, out=w_out,
        b_out=b_out, gain1=gain_attn, shift1=bias_attn, inner=w_inner, b_inner=b_inner,
        outer=w_outer, b_outer=b_outer, gain2=gain_ffn, shift2=bias_ffn,
    )
    x = tokens[0]
    seg = segments[0]
    order = list(range(bits - 1, 1, -1)) + ["xy", "yx", "core"]
    singles = [b_query, b_value, b_out, gain_attn, bias_attn, b_outer, gain_ffn, bias_ffn, b_inner]
    (
        q, k, v, mixed, stat, first_low, normed1, act, slope, normed2, hidden, pooled, unit, vectors
    ) = forward(x, seg, singles, w)
    every = gather_all(unit, steps, order)
    loss, unit_grad, pooled_grad = contrast(
        order, bits, counts, every, unit, pooled, seg
    )
    loss = loss[:, 0].reshape(1, batches, SLOTS)
    d2, grad_h2, sums2 = norm2_backward(cotangent[0], normed2, stat, seg, pooled_grad, vectors)

    tokens_all = batches * length
    flat = lambda a: a.reshape(tokens_all, a.shape[-1])
    core = steps["core"][0].reshape(1).astype(jnp.int32)
    line = Line(
        d2=flat(d2), act=flat(act), slope=flat(slope), h2=grad_h2, first=flat(first_low),
        normed1=normed1, q=q,
    )
    middle = list(range(3, bits - 1))
    flat_route = ["core", "xy", "yx", 2] + middle
    deep_route = ["core", 2, "yx", "xy"] + middle
    last = bits - 1
    blocks = 1 << len(flat_route)
    outer = Sum(line, "outer", steps, flat_route, last, False, "total_outer")
    inner = Sum(line, "inner", steps, flat_route, last, True, "total_inner")
    rest = PairSum(
        line, "rest", steps, (flat_route, deep_route), last,
        lambda k, g, b: join_attention(k, g, b, blocks // 2),
        ["total_query", "total_key", "total_value", "total_out", "vectors"],
    )
    xf, mixed_f = flat(x), flat(mixed)

    def give(group, function, given):
        name = group.name + ".give"
        line.step(lambda *a: (function(*a, 1 - core),), given, [name])
        if group is rest:
            group.start(line.at[name], split_attention(line.at[name].shape[0], blocks // 2))
        else:
            group.start(line.at[name])

    def keep(group, function, given):
        line.step(lambda *a: (function(*a, core),), given, [group.name + ".keep"])

    def inner_step(d2, slope):
        grad_inner = matmul_nt(d2, w_outer) * slope.astype(F32)
        return grad_inner.astype(BF16), jnp.sum(grad_inner, axis=0, keepdims=True)

    def first_step(d1, h2, normed):
        d1 = d1.reshape(batches, length, ff)
        h1, d0, dm, sums = first_backward(h2, d1, normed, stat, vectors, w_inner, w_out)
        return flat(h1), flat(d0), dm, sums

    def attention(batch):
        names = ["dq", "dk", "dv", "sums0"]
        into = names if batch else []
        line.step(
            lambda q, dm, *into: attention_backward(q, k, v, dm, stat, seg, batch, into),
            ["q", "dm"] + into, names,
        )

    def attention_grads(d0, dq, dk, dv, vectors, half):
        return attention_grad_half(xf, mixed_f, flat(dq), flat(dk), flat(dv), d0, vectors, half)

    attention_given = ["d0", "dq", "dk", "dv", "vec"]

    def token_gradient(h1, dq, dk, dv):
        return (
            (
                h1
                + matmul_nt(flat(dq), w_query)
                + matmul_nt(flat(dk), w_key)
                + matmul_nt(flat(dv), w_value)
            ).astype(BF16),
        )

    def vector_step():
        line.step(
            lambda a, b, c: (pack_vectors(a, b, sums2, c, blocks),), ["sums0", "sums1", "b_inner"], ["vec"]
        )

    actions = {
        "gw1s": lambda: give(outer, outer_grad_half, ["act", "d2"]),
        "gw1k": lambda: outer.keep_and_split(True, ["act", "d2"]),
        "B2": lambda: line.step(inner_step, ["d2", "slope"], ["d1", "b_inner"]),
        "gw2s": lambda: give(inner, inner_grad_half, ["first", "d1"]),
        "gw2k": lambda: inner.keep_and_split(False, ["first", "d1"]),
        "B3": lambda: line.step(first_step, ["d1", "h2", "normed1"], ["h1", "d0", "dm", "sums1"]),
        "at0": lambda: attention(0),
        "at1": lambda: attention(1),
        "gw3s": lambda: give(rest, attention_grads, attention_given),
        "gw3k": lambda: keep(rest, attention_grads, attention_given),
        "tok": lambda: line.step(token_gradient, ["h1", "dq", "dk", "dv"], ["tokens"]),
        "v": vector_step,
        "0": outer.visit,
        "1": inner.visit,
        "2": rest.visit,
    }
    for action in ORDER:
        actions[action]()
    for group in (inner, outer, rest):
        while group.visits < 2 * len(flat_route) + 1:
            group.visit()
    total = line.at
    sums = total["vectors"]
    return (
        loss,
        unit.reshape(1, batches, SLOTS, D),
        unit_grad.reshape(1, batches, SLOTS, D),
        hidden[None],
        total["tokens"].reshape(1, batches, length, D),
        total["total_query"],
        sums[0],
        total["total_key"],
        total["total_value"],
        sums[1],
        total["total_out"],
        sums[2],
        sums[3],
        sums[4],
        total["total_inner"],
        sums[8 : 8 + ff // D].reshape(ff),
        total["total_outer"],
        sums[5],
        sums[6],
        sums[7],
    )


def solution(mesh):
    row = P("stream", None, "pairs", None)
    in_specs = (row, row, P(), row) + (P(),) * 15
    out_specs = (P("stream", None, "pairs"), row, row, row, row) + (P(),) * 15
    return jax.shard_map(
        on_device, mesh=mesh, in_specs=in_specs, out_specs=out_specs, check_vma=False
    )
```
